256 devices in a mesh: slab: 16 (over z, core), pencil: 16 (over y, x).
Axes of the slice: x: 4, y: 4, z: 8, core: 2. Of those that a mesh axis runs over, the one named last changes fastest.
Arguments:
- fractions: float32 [3, 4194304], P(None, ('slab', 'pencil')), may hold values from 0 to 1
- cell_index: int32 [3, 4194304], P(None, ('slab', 'pencil')), may hold values from 0 to 63, as said below
- weights: bfloat16 [4, 4194304], P(None, ('slab', 'pencil')), may hold values from -6 to 6
- counts: int32 [256, 256, 32], P(('slab', 'pencil')), may hold values from 0 to 2, as said below
- smoothing: float32 [4], replicated, may hold values from 1 to 256
- bias_values: float32 [4], replicated, may hold values from 0.5 to 1.5
- observed: float32 [16, 1024, 1024], P('slab', 'pencil'), may hold values from -6 to 6
- precision: float32 [16, 1024, 1024], P('slab', 'pencil'), may hold values from 0.25 to 4
Outputs:
- particle_grads: float32 [7, 4194304], P(None, ('slab', 'pencil'))
- model_field: bfloat16 [16, 1024, 1024], P('slab', 'pencil')
The draws below stay inside these ranges and needn't reach their ends.
Inputs may be any that keep to these rules, and one draw needn't show every extreme that they name: counts[s, t, b] is how many of the 2 slots that device s holds for z block b of tile t are live (the first ones); some tile gets 2 for every block from every device. `cell_index`: row 0 is below 1, row 1 below 64, row 2 below 32.
All inputs are finite; a program needn't handle non-finite values.
Results may differ from the reference program's by a relative error of at most 0.0074.
Values may be sent and summed in bfloat16 or wider, within the bound.
No kernel may reach another device: no remote copies, remote signals or barrier semaphores. Data moves between devices by JAX's collectives and lax.ppermute only.
A program may use at most 128 MiB of HBM per device.

```python
import math
import jax
import jax.numpy as jnp
from jax import lax

TX = 1
NY = 1024
NZ = 1024
C = 4
ZB = 32
PART_DEV = 16384
TILES = 256
NX = 16
TY = 64
ZBLK = 32
CAP = 2
N_PENCIL = 16


def draw_cell_index(key, part):
    key_x, key_y, key_z = jax.random.split(key, 3)
    slot_total = TILES * PART_DEV
    along_x = jax.random.randint(key_x, (1, slot_total), 0, TX)
    along_y = jax.random.randint(key_y, (1, slot_total), 0, TY)
    along_z = jax.random.randint(key_z, (1, slot_total), 0, ZB)
    return jnp.concatenate([along_x, along_y, along_z], axis=0).astype(jnp.int32)


def draw_counts(key, part):
    key_light, key_heavy, key_forced = jax.random.split(key, 3)
    light_load = jax.random.randint(key_light, (TILES, TILES, ZBLK), 0, CAP)
    picked = jax.random.randint(key_heavy, (TILES,), 0, 8) == 0
    forced = jnp.arange(TILES) == jax.random.randint(key_forced, (), 0, TILES)
    heavy_tile = jnp.logical_or(picked, forced)
    return jnp.where(heavy_tile[None, :, None], CAP, light_load).astype(jnp.int32)


def draw_smoothing(key, part):
    key_stratum, key_jitter = jax.random.split(key, 2)
    stratum = jax.random.permutation(key_stratum, C).astype(jnp.float32)
    jitter = jax.random.uniform(key_jitter, (C,), jnp.float32)
    position = (stratum + jitter) / C
    return jnp.exp(position * math.log(NY / 4.0)).astype(jnp.float32)


def draw_observed(key, part):
    key_rough = jax.random.fold_in(key, 0)
    extent_all = (NX, NZ, NY)
    return jnp.clip(jax.random.normal(key_rough, extent_all, jnp.float32), -6.0, 6.0)


def shard_levels(own_key, dims, cuts, least, top_value):
    loudness = 1.0
    for axis_at, shards_of in cuts:
        steps = jax.random.uniform(jax.random.fold_in(jax.random.fold_in(own_key, 6), axis_at), (shards_of,), jnp.float32, least / len(cuts), top_value / len(cuts))
        loudness = loudness * jnp.repeat(jnp.exp(steps), dims[axis_at] // shards_of).reshape((-1,) + (1,) * (len(dims) - 1 - axis_at))
    return loudness


def scatter_about(rng, dims, width, most, cuts=(), kind=jnp.bfloat16):
    drawn = width * jax.random.normal(rng, dims, jnp.float32)
    if cuts:
        drawn = drawn * shard_levels(rng, dims, cuts, -0.22, 0.18)
    return jnp.clip(drawn, -most, most).astype(kind)


def setup_inputs(seed: int = 0) -> dict:
    key_of = jax.random.split(jax.random.key(seed), 9)
    fractions = jnp.clip(1.0 * jax.random.uniform(key_of[0], (3, TILES * PART_DEV), jnp.float32) ** shard_levels(key_of[0], (3, TILES * PART_DEV), ((1, 256),), -0.2, 0.2), 0.0, 1.0)
    cell_index = draw_cell_index(jax.random.fold_in(key_of[8], 71), 0)
    weights = scatter_about(key_of[2], (C, TILES * PART_DEV), 1.0, 6.0, ((1, 256),))
    counts = draw_counts(jax.random.fold_in(key_of[8], 71), 0)
    smoothing = draw_smoothing(jax.random.fold_in(key_of[8], 71), 0)
    bias_values = jnp.clip(jax.random.uniform(key_of[5], (C,), jnp.float32, 0.5, 1.5), 0.5, 1.5)
    observed = draw_observed(jax.random.fold_in(key_of[8], 71), 0)
    precision = jnp.clip(jnp.exp(math.log(4.0) - 2.7725887 * jax.random.uniform(key_of[7], (NX, NZ, NY), jnp.float32) ** shard_levels(key_of[7], (NX, NZ, NY), ((0, 16), (1, 16)), -0.2, 0.2)), 0.25, 4.0)
    return {"fractions": fractions, "cell_index": cell_index, "weights": weights, "counts": counts, "smoothing": smoothing, "bias_values": bias_values, "observed": observed, "precision": precision}


def rounded(values):
    return lax.optimization_barrier(values.astype(jnp.bfloat16)).astype(jnp.float32)

def kernel_matrix(breadth, extent):
    places = jnp.arange(extent, dtype=jnp.int32)
    distance = jnp.abs(places[:, None] - places[None, :])
    distance = jnp.minimum(distance, extent - distance).astype(jnp.float32)
    profile = jnp.exp(-distance * distance / (2.0 * breadth * breadth)) / jnp.sqrt(breadth)
    return (profile + jnp.where(distance == 0.0, 1.0, 0.0)).astype(jnp.bfloat16)

def cloud_table(fraction):
    falling = fraction < 0.5
    weights_1d = [jnp.maximum(0.5 - fraction, 0.0), 1.0 - jnp.abs(fraction - 0.5), jnp.maximum(fraction - 0.5, 0.0)]
    slopes_1d = [jnp.where(falling, -1.0, 0.0), jnp.where(falling, 1.0, -1.0), jnp.where(falling, 0.0, 1.0)]
    return (weights_1d, slopes_1d)

def reference(fractions, cell_index, weights, counts, smoothing, bias_values, observed, precision):
    slot_total = TILES * PART_DEV
    slot_index = jnp.arange(slot_total, dtype=jnp.int32)
    source = slot_index // PART_DEV
    on_device = slot_index % PART_DEV
    tile_index = on_device // (ZBLK * CAP)
    block_index = on_device // CAP % ZBLK
    slot_rank = on_device % CAP
    live_mask = (slot_rank < counts[source, tile_index, block_index]).astype(jnp.float32)
    masses = weights.astype(jnp.float32) * live_mask[None, :]
    grid_x = tile_index // N_PENCIL * TX + cell_index[0]
    grid_y = tile_index % N_PENCIL * TY + cell_index[1]
    grid_z = block_index * ZB + cell_index[2]
    weight_x, slope_x = cloud_table(fractions[0])
    weight_y, slope_y = cloud_table(fractions[1])
    weight_z, slope_z = cloud_table(fractions[2])
    cells_x = [(grid_x + step - 1) % NX for step in range(3)]
    cells_y = [(grid_y + step - 1) % NY for step in range(3)]
    cells_z = [(grid_z + step - 1) % NZ for step in range(3)]
    highest = lax.Precision.HIGHEST
    model_values = jnp.zeros((NX, NZ, NY), jnp.float32)
    for channel in range(C):
        flat_field = jnp.zeros((NX * NY * NZ,), jnp.float32)
        for step_x in range(3):
            for step_y in range(3):
                plane_w = rounded(weight_x[step_x] * weight_y[step_y])
                for step_z in range(3):
                    column_w = rounded(masses[channel] * weight_z[step_z])
                    target = (cells_x[step_x] * NY + cells_y[step_y]) * NZ + cells_z[step_z]
                    flat_field = flat_field.at[target].add(plane_w * column_w)
        density = flat_field.reshape(NX, NY, NZ).astype(jnp.bfloat16)
        kernel_y = kernel_matrix(smoothing[channel], NY).astype(jnp.float32)
        kernel_z = kernel_matrix(smoothing[channel], NZ).astype(jnp.float32)
        smooth_z = jnp.einsum('xyz,zw->xyw', density.astype(jnp.float32), kernel_z, precision=highest).astype(jnp.bfloat16)
        model_values = model_values + bias_values[channel] * jnp.einsum('xyz,yw->xzw', smooth_z.astype(jnp.float32), kernel_y, precision=highest)
    model_field = model_values.astype(jnp.bfloat16)
    pull_field = rounded(precision * (model_values - observed))
    grad_rows = []
    grad_x = jnp.zeros((slot_total,), jnp.float32)
    grad_y = jnp.zeros((slot_total,), jnp.float32)
    grad_z = jnp.zeros((slot_total,), jnp.float32)
    for channel in range(C):
        kernel_y = kernel_matrix(smoothing[channel], NY).astype(jnp.float32)
        kernel_z = kernel_matrix(smoothing[channel], NZ).astype(jnp.float32)
        returned_y = rounded(bias_values[channel] * jnp.einsum('xzy,yw->xwz', pull_field, kernel_y, precision=highest))
        adjoint = rounded(jnp.einsum('xyz,zw->xyw', returned_y, kernel_z, precision=highest)).reshape(-1)
        grad_mass = jnp.zeros((slot_total,), jnp.float32)
        for step_x in range(3):
            for step_y in range(3):
                plane_w = rounded(weight_x[step_x] * weight_y[step_y])
                slope_xw = rounded(slope_x[step_x] * weight_y[step_y])
                slope_yw = rounded(weight_x[step_x] * slope_y[step_y])
                for step_z in range(3):
                    target = (cells_x[step_x] * NY + cells_y[step_y]) * NZ + cells_z[step_z]
                    sampled = adjoint[target]
                    grad_mass = grad_mass + plane_w * sampled * weight_z[step_z]
                    grad_x = grad_x + masses[channel] * slope_xw * sampled * weight_z[step_z]
                    grad_y = grad_y + masses[channel] * slope_yw * sampled * weight_z[step_z]
                    grad_z = grad_z + masses[channel] * plane_w * sampled * slope_z[step_z]
        grad_rows.append(grad_mass)
    particle_grads = jnp.stack(grad_rows + [grad_x, grad_y, grad_z]) * live_mask[None, :]
    return (particle_grads, model_field)
```

```python
import jax
import jax.numpy as jnp
from jax import lax
from jax.experimental import pallas as pl
from jax.experimental.pallas import tpu as pltpu
from jax.sharding import PartitionSpec as P

NY = 1024
NZ = 1024
ZB = 32
PART_DEV = 16384
TILES = 256
CAP = 2
TY = 64
LANES = 64
RECORD = 12 * LANES
GRADS = 7 * LANES
CH = 4
N_PENCIL = 16
CHUNK = 136
F32 = jnp.float32
BF16 = jnp.bfloat16

R_GX, R_GY, R_GZ, R_LOW, R_CY, R_CZ = 4, 5, 6, 3, 10, 11


def params():
    return pltpu.CompilerParams(vmem_limit_bytes=56 * 1024 * 1024)


def lanes_of(shape):
    return lax.broadcasted_iota(jnp.int32, shape, len(shape) - 1)


def live_table(counts_ref):
    lane = lanes_of((ZB, 128))
    block = lax.broadcasted_iota(jnp.int32, (ZB, 128), 0)
    spread = jnp.where((lane % LANES) // CAP == block, 1.0, 0.0).astype(BF16)
    held = jnp.dot(counts_ref[...].astype(F32).astype(BF16), spread, preferred_element_type=F32)
    rank = (lanes_of((TILES, 128)) % CAP).astype(F32)
    return rank < held


def pack_kernel(fr_ref, ci_ref, wt_ref, cn_ref, out_ref, scr):
    low = lanes_of((128, 128)) < LANES

    def put(j, a, b):
        even = jnp.where(low, a, pltpu.roll(b, LANES, 1))
        odd = jnp.where(low, pltpu.roll(a, LANES, 1), b)
        scr[j, pl.ds(0, 128, stride=2), :] = even
        scr[j, pl.ds(1, 128, stride=2), :] = odd

    put(0, wt_ref[0].astype(F32), wt_ref[1].astype(F32))
    put(1, wt_ref[2].astype(F32), wt_ref[3].astype(F32))
    offsets = [fr_ref[d] - 0.5 for d in range(3)]
    high = [g.astype(BF16).astype(F32) for g in offsets]
    rest = [g - h for g, h in zip(offsets, high)]
    put(2, high[0], high[1])
    put(3, high[2], rest[0])
    put(4, rest[1], rest[2])
    put(5, ci_ref[1].astype(F32), ci_ref[2].astype(F32))
    live = live_table(cn_ref)
    out_ref[:, 0:128] = jnp.where(live, scr[0], 0.0).astype(BF16)
    out_ref[:, 128:256] = jnp.where(live, scr[1], 0.0).astype(BF16)
    for j in range(2, 6):
        out_ref[:, j * 128 : j * 128 + 128] = scr[j].astype(BF16)


def unpack_kernel(in_ref, cn_ref, out_ref, scr):
    live = live_table(cn_ref)
    low = lanes_of((128, 128)) < LANES
    for j in range(4):
        if j < 3:
            scr[...] = jnp.where(live, in_ref[:, j * 128 : j * 128 + 128].astype(F32), 0.0)
        else:
            scr[:, 0:LANES] = jnp.where(live[:, 0:LANES], in_ref[:, 384:GRADS].astype(F32), 0.0)
        even = scr[pl.ds(0, 128, stride=2), :]
        odd = scr[pl.ds(1, 128, stride=2), :]
        out_ref[2 * j] = jnp.where(low, even, pltpu.roll(odd, LANES, 1))
        if j < 3:
            out_ref[2 * j + 1] = jnp.where(low, pltpu.roll(even, LANES, 1), odd)


def transpose_records(x_ref, xt_ref):
    for j in range(6):
        for h in range(2):
            piece = x_ref[h * 128 : h * 128 + 128, j * 128 : j * 128 + 128].astype(F32)
            xt_ref[j * 128 : j * 128 + 128, h * 128 : h * 128 + 128] = piece.T
    first, last = R_GX * LANES, R_GZ * LANES + LANES
    xt_ref[first:last, :] += xt_ref[first + R_LOW * LANES : last + R_LOW * LANES, :]


def slot_row(xt_ref, r, b):
    first = xt_ref[pl.ds(r * LANES + 2 * b, 1), :]
    second = xt_ref[pl.ds(r * LANES + 2 * b + 1, 1), :]
    return jnp.concatenate([first, second], axis=1)


def hat(places, centre):
    return jnp.maximum(1.0 - jnp.abs(places - centre), 0.0)


def rim_places(rows):
    row = lax.broadcasted_iota(jnp.int32, (rows, 128), 0)
    y = jnp.where(row == 64, -1, jnp.where(row == 65, 64, jnp.where(row > 65, 1000, row)))
    return y.astype(F32)


def deposit(xt_ref, acc_ref, yv_ref, zv_ref, side):
    def block(b, carry):
        gx = slot_row(xt_ref, R_GX, b)
        if side == 0:
            wx = 1.0 - jnp.abs(gx)
        elif side < 0:
            wx = jnp.maximum(-gx, 0.0)
        else:
            wx = jnp.maximum(gx, 0.0)
        py = slot_row(xt_ref, R_CY, b) + slot_row(xt_ref, R_GY, b)
        pz = slot_row(xt_ref, R_CZ, b) + slot_row(xt_ref, R_GZ, b) + 8.0
        plane = (wx * hat(yv_ref[...], py)).astype(BF16)
        wz = hat(zv_ref[...], pz)
        column = jnp.concatenate([slot_row(xt_ref, c, b) * wz for c in range(CH)], axis=0).astype(BF16)
        add = lax.dot_general(column, plane, (((1,), (1,)), ((), ())), preferred_element_type=F32)
        at = pl.multiple_of(b * ZB, ZB)
        for c in range(CH):
            acc_ref[c, pl.ds(at, 48), 0:72] += add[c * 48 : c * 48 + 48]
        return carry

    lax.fori_loop(0, NZ // ZB, block, 0, unroll=2)


def fill_places(yv_ref, zv_ref):
    yv = rim_places(72)
    zv = lax.broadcasted_iota(jnp.int32, (48, 128), 0).astype(F32)
    for k in range(4):
        yv_ref[:, k * 128 : k * 128 + 128] = yv
        zv_ref[:, k * 128 : k * 128 + 128] = zv


def own_kernel(x_ref, acc_ref, xt_ref, yv_ref, zv_ref):
    fill_places(yv_ref, zv_ref)
    transpose_records(x_ref, xt_ref)
    acc_ref[...] = jnp.zeros_like(acc_ref)
    deposit(xt_ref, acc_ref, yv_ref, zv_ref, 0)


def along_z(field_ref, col_ref, out_ref):
    def channel(c, carry):
        for half in range(2):
            pair = jnp.concatenate(
                [
                    field_ref[c, (2 * half) * 256 : (2 * half) * 256 + 256, :],
                    field_ref[c, (2 * half + 1) * 256 : (2 * half + 1) * 256 + 256, :],
                ],
                axis=1,
            )
            prods = [
                jnp.dot(col_ref[c, d * 256 : d * 256 + 256, :], pair, preferred_element_type=F32)
                for d in range(4)
            ]
            for j in range(4):
                part = prods[(j - 2 * half) % 4][:, 0:128] + prods[(j - 2 * half - 1) % 4][:, 128:256]
                if half == 0:
                    out_ref[c, j * 256 : j * 256 + 256, :] = part
                else:
                    out_ref[c, j * 256 : j * 256 + 256, :] += part
        return carry

    lax.fori_loop(0, CH, channel, 0)


def rim_rows(parts, rows):
    lane = lanes_of((rows, 128))
    table = jnp.zeros((rows, 128), F32)
    for c in range(CH):
        table = jnp.where(lane // 2 == c, pltpu.roll(parts[c], LANES + 2 * c, 1), table)
    return table.T[0:8]


def forward_kernel(up_ref, dn_ref, start_ref, col_ref, out_ref, acc, xt, yv, zv, dens, smooth):
    fill_places(yv, zv)
    acc[...] = start_ref[...]
    transpose_records(up_ref, xt)
    deposit(xt, acc, yv, zv, 1)
    transpose_records(dn_ref, xt)
    deposit(xt, acc, yv, zv, -1)
    acc[:, 1024:1032, :] += jnp.concatenate(
        [jnp.zeros((CH, 7, 128), F32), acc[:, 7:8, :]], axis=1
    )
    acc[:, 8:16, :] += jnp.concatenate([acc[:, 1032:1033, :], jnp.zeros((CH, 7, 128), F32)], axis=1)
    dens[...] = acc[:, 8:1032, :].astype(BF16)
    along_z(dens, col_ref, smooth)
    low = lanes_of((64, 128)) < LANES

    def send(p, carry):
        at = pl.multiple_of(p * 64, 64)
        parts = [smooth[c, pl.ds(at, 64), :] for c in range(CH)]
        for pair in range(2):
            both = jnp.where(low, parts[2 * pair], pltpu.roll(parts[2 * pair + 1], LANES, 1))
            out_ref[p, pair * 64 : pair * 64 + 64, :] = both.astype(BF16)
        rims = rim_rows(parts, 64)
        out_ref[p, 128:136, :] = jnp.concatenate([rims, jnp.zeros((8, 64), F32)], axis=1).astype(BF16)
        return carry

    lax.fori_loop(0, N_PENCIL, send, 0)


def wrapped_sum(prod):
    blocks = []
    for j in range(4):
        total = prod[0:64, j * 256 : j * 256 + 256]
        for i in range(1, 4):
            d = (j - i) % 4
            total = total + prod[i * 64 : i * 64 + 64, d * 256 : d * 256 + 256]
        blocks.append(total)
    return jnp.concatenate(blocks, axis=1)


def lines_kernel(bias_ref, in_ref, row_ref, rim_ref, obs_ref, prec_ref, model_ref, out_ref, left, back):
    low = lanes_of((64, 128)) < LANES
    for pair in range(2):
        for pp in range(8):
            a = in_ref[2 * pp, pair * 64 : pair * 64 + 64, :].astype(F32)
            b = in_ref[2 * pp + 1, pair * 64 : pair * 64 + 64, :].astype(F32)
            i, at = pp // 2, (pp % 2) * 128
            left[2 * pair, i * 64 : i * 64 + 64, at : at + 128] = jnp.where(
                low, a, pltpu.roll(b, LANES, 1)
            ).astype(BF16)
            left[2 * pair + 1, i * 64 : i * 64 + 64, at : at + 128] = jnp.where(
                low, pltpu.roll(a, LANES, 1), b
            ).astype(BF16)
    which = lax.broadcasted_iota(jnp.int32, (128, 64), 0) % 8 // 2
    bias = jnp.zeros((128, 64), F32)
    for c in range(CH):
        bias = jnp.where(which == c, bias_ref[c], bias)
    rims = jnp.concatenate([in_ref[p, 128:136, 0:64].astype(F32) for p in range(N_PENCIL)], axis=0)
    rims = (rims * bias).T.astype(BF16)
    model = jnp.dot(rims, rim_ref[...], preferred_element_type=F32)
    for c in range(CH):
        prod = jnp.dot(left[c], row_ref[c], preferred_element_type=F32)
        model = model + bias_ref[c] * wrapped_sum(prod)
    model_ref[...] = model.astype(BF16)
    pull = (prec_ref[...] * (model - obs_ref[...])).astype(BF16)
    stacked = jnp.concatenate([pull[:, i * 256 : i * 256 + 256] for i in range(4)], axis=0)
    for c in range(CH):
        prod = jnp.dot(stacked, row_ref[c], preferred_element_type=F32)
        back[c] = bias_ref[c] * wrapped_sum(prod)
    for pair in range(2):
        for pp in range(8):
            a = back[2 * pair, :, pp * 128 : pp * 128 + 128]
            b = back[2 * pair + 1, :, pp * 128 : pp * 128 + 128]
            out_ref[2 * pp, pair * 64 : pair * 64 + 64, :] = jnp.where(
                low, a, pltpu.roll(b, LANES, 1)
            ).astype(BF16)
            out_ref[2 * pp + 1, pair * 64 : pair * 64 + 64, :] = jnp.where(
                low, pltpu.roll(a, LANES, 1), b
            ).astype(BF16)
    rims = lax.dot_general(rim_ref[...], pull, (((1,), (1,)), ((), ())), preferred_element_type=F32)
    rims = jnp.concatenate([rims * bias, jnp.zeros((128, 64), F32)], axis=1).astype(BF16)
    for p in range(N_PENCIL):
        out_ref[p, 128:136, :] = rims[p * 8 : p * 8 + 8]


def adjoint_kernel(in_ref, col_ref, out_ref, field, smooth):
    lane = lanes_of((64, 128))
    low = lane < LANES

    def take(p, carry):
        at = pl.multiple_of(p * 64, 64)
        rims = in_ref[p, 128:136, :].astype(F32)
        table = jnp.concatenate([rims, jnp.zeros((120, 128), F32)], axis=0).T[0:64]
        for pair in range(2):
            both = in_ref[p, pair * 64 : pair * 64 + 64, :].astype(F32)
            for k in range(2):
                c = 2 * pair + k
                main = both if k == 0 else pltpu.roll(both, LANES, 1)
                rim = jnp.where(lane < 66, pltpu.roll(table, LANES - 2 * c, 1), 0.0)
                field[c, pl.ds(at, 64), :] = jnp.where(low, main, rim).astype(BF16)
        return carry

    lax.fori_loop(0, N_PENCIL, take, 0)
    along_z(field, col_ref, smooth)
    wide = lanes_of((128, 128)) < LANES
    for q in range(8):
        parts = [smooth[c, q * 128 : q * 128 + 128, :] for c in range(CH)]
        for pair in range(2):
            both = jnp.where(wide, parts[2 * pair], pltpu.roll(parts[2 * pair + 1], LANES, 1))
            out_ref[pair * 1024 + q * 128 : pair * 1024 + q * 128 + 128, :] = both.astype(BF16)
        out_ref[2048 + q * 8 : 2048 + q * 8 + 8, :] = rim_rows(parts, 128).astype(BF16)


def sample_kernel(xt_ref, own_ref, up_ref, dn_ref, out_ref, field, planes, yv, ot):
    lane = lanes_of((128, 128))
    low = lane < LANES

    def fill(q, carry):
        at = pl.multiple_of(q * 128, 128)
        to = pl.multiple_of(q * 128 + 16, 16)
        rim_at = pl.multiple_of(2048 + q * 8, 8)
        tables = []
        for ref in (own_ref, up_ref, dn_ref):
            rims = ref[pl.ds(rim_at, 8), :].astype(F32)
            tables.append(jnp.concatenate([rims, jnp.zeros((120, 128), F32)], axis=0).T)
        for pair in range(2):
            own = own_ref[pl.ds(pair * 1024 + at, 128), :].astype(F32)
            up = up_ref[pl.ds(pair * 1024 + at, 128), :].astype(F32)
            dn = dn_ref[pl.ds(pair * 1024 + at, 128), :].astype(F32)
            for k in range(2):
                c = 2 * pair + k
                if k == 0:
                    first = jnp.where(low, up, pltpu.roll(dn, LANES, 1))
                    main = own
                else:
                    first = jnp.where(low, pltpu.roll(up, LANES, 1), dn)
                    main = pltpu.roll(own, LANES, 1)
                rim = jnp.zeros((128, 128), F32)
                for s in range(3):
                    here = pltpu.roll(tables[s], LANES + 2 * s - 2 * c, 1)
                    rim = jnp.where((lane - LANES) // 2 == s, here, rim)
                field[c, pl.ds(to, 128), 0:128] = first.astype(BF16)
                field[c, pl.ds(to, 128), 128:256] = jnp.where(low, main, rim).astype(BF16)
        return carry

    lax.fori_loop(0, 8, fill, 0)
    field[:, 0:16, :] = field[:, 1024:1040, :]
    field[:, 1040:1056, :] = field[:, 16:32, :]
    planes[...] = jnp.zeros_like(planes)
    row = lax.broadcasted_iota(jnp.int32, (72, 512), 0)
    yv[...] = jnp.where(row < 64, row, jnp.where(row % 2 == 0, -1, 64)).astype(F32)
    zv = (lax.broadcasted_iota(jnp.int32, (48, 512), 0) + 8).astype(F32)
    part = lax.broadcasted_iota(jnp.int32, (8, 512), 0) // 2

    def block(b, carry):
        gx, gy, gz = (slot_row(xt_ref, r, b) for r in (R_GX, R_GY, R_GZ))
        cy, cz = slot_row(xt_ref, R_CY, b), slot_row(xt_ref, R_CZ, b)
        fall_x, fall_y, fall_z = gx < 0.0, gy < 0.0, gz < 0.0
        wx = [jnp.maximum(-gx, 0.0), jnp.maximum(gx, 0.0), 1.0 - jnp.abs(gx)]
        sx = [jnp.where(fall_x, -1.0, 0.0), jnp.where(fall_x, 0.0, 1.0), jnp.where(fall_x, 1.0, -1.0)]
        places = yv[...]
        wy = hat(places, cy + gy)
        step_y = places - jnp.where(fall_y, cy - 1.0, cy)
        sy = jnp.where(step_y == 0.0, -1.0, jnp.where(step_y == 1.0, 1.0, 0.0))
        for k, (ax, ay) in enumerate(((wx, wy), (sx, wy), (wx, sy))):
            cols = slice(k * 512, k * 512 + 512)
            for s in range(3):
                planes[s * 64 : s * 64 + 64, cols] = (ax[s] * ay[0:64]).astype(BF16)
            rim = jnp.where(
                part == 0, ax[2], jnp.where(part == 1, ax[0], jnp.where(part == 2, ax[1], 0.0))
            )
            rim = rim * ay[64:72]
            planes[192:208, cols] = jnp.concatenate([rim, jnp.zeros((8, 512), F32)], axis=0).astype(BF16)
        at = pl.multiple_of(b * ZB, ZB)
        here = jnp.concatenate([field[c, pl.ds(at, 64), :] for c in range(CH)], axis=0)
        wz = hat(zv, cz + gz + 16.0)
        step_z = zv - jnp.where(fall_z, cz + 15.0, cz + 16.0)
        sz = jnp.where(step_z == 0.0, -1.0, jnp.where(step_z == 1.0, 1.0, 0.0))
        masses = [slot_row(xt_ref, c, b) for c in range(CH)]
        values = jnp.dot(here, planes[:, 0:512], preferred_element_type=F32)
        grads = []
        slope_z = jnp.zeros((1, 512), F32)
        for c in range(CH):
            v = values[c * 64 + 8 : c * 64 + 56]
            grads.append(jnp.sum(v * wz, axis=0, keepdims=True))
            slope_z = slope_z + masses[c] * jnp.sum(v * sz, axis=0, keepdims=True)
        for k in (1, 2):
            slopes = jnp.dot(here, planes[:, k * 512 : k * 512 + 512], preferred_element_type=F32)
            total = jnp.zeros((48, 512), F32)
            for c in range(CH):
                total = total + masses[c] * slopes[c * 64 + 8 : c * 64 + 56]
            grads.append(jnp.sum(total * wz, axis=0, keepdims=True))
        grads.append(slope_z)
        for r in range(7):
            ot[pl.ds(r * LANES + 2 * b, 1), :] = grads[r][:, 0:256]
            ot[pl.ds(r * LANES + 2 * b + 1, 1), :] = grads[r][:, 256:512]
        return carry

    lax.fori_loop(0, NZ // ZB, block, 0, unroll=2)
    for j in range(4):
        wide = 128 if j < 3 else LANES
        for h in range(2):
            piece = ot[j * 128 : j * 128 + wide, h * 128 : h * 128 + 128]
            out_ref[h * 128 : h * 128 + 128, j * 128 : j * 128 + wide] = piece.T.astype(BF16)


def correlation(smoothing, rows, columns):
    distance = jnp.abs(rows - columns)
    distance = jnp.minimum(distance, NY - distance).astype(F32)
    breadth = smoothing
    profile = jnp.exp(-distance * distance / (2.0 * breadth * breadth)) / jnp.sqrt(breadth)
    return (profile + jnp.where(distance == 0.0, 1.0, 0.0)).astype(BF16)


def call(kernel, outs, scratch, cost=None):
    return pl.pallas_call(
        kernel,
        out_shape=outs,
        scratch_shapes=scratch,
        compiler_params=params(),
        cost_estimate=cost,
    )


def shape(dims, kind):
    return jax.ShapeDtypeStruct(dims, kind)


def per_device(fractions, cell_index, weights, counts, smoothing, bias_values, observed, precision):
    both = ("slab", "pencil")
    count = lax.axis_size("slab")
    forth = [(i, (i + 1) % count) for i in range(count)]
    aft = [((i + 1) % count, i) for i in range(count)]

    ids = jnp.arange(NY, dtype=jnp.int32)
    breadth = smoothing[:, None, None]
    k_row = correlation(breadth, ids[None, :256, None], ids[None, None, :])
    k_col = correlation(breadth, ids[None, :, None], ids[None, None, :256])
    rim = jnp.arange(128, dtype=jnp.int32)
    rim_y = (rim // 8 * TY - 1 + rim % 2 * (TY + 1)) % NY
    k_rim = correlation(smoothing[rim % 8 // 2][:, None], rim_y[:, None], ids[None, :])

    table = counts[0]
    records = call(pack_kernel, shape((TILES, RECORD), BF16), [pltpu.VMEM((6, TILES, 128), F32)])(
        fractions.reshape(3, 128, 128),
        cell_index.reshape(3, 128, 128),
        weights.reshape(CH, 128, 128),
        table,
    )
    arrived = lax.all_to_all(records, both, split_axis=0, concat_axis=0, tiled=True)
    from_up = lax.ppermute(arrived, "slab", forth)
    from_dn = lax.ppermute(arrived, "slab", aft)
    places = [pltpu.VMEM((72, 512), F32), pltpu.VMEM((48, 512), F32)]
    acc, turned = call(
        own_kernel, (shape((CH, 1040, 128), F32), shape((RECORD, TILES), F32)), places
    )(arrived)
    lines = call(
        forward_kernel,
        shape((N_PENCIL, CHUNK, 128), BF16),
        [pltpu.VMEM((CH, 1040, 128), F32), pltpu.VMEM((RECORD, TILES), F32)]
        + places
        + [pltpu.VMEM((CH, NZ, 128), BF16), pltpu.VMEM((CH, NZ, 128), F32)],
    )(from_up, from_dn, acc, k_col)
    lines = lax.all_to_all(lines, "pencil", split_axis=0, concat_axis=0, tiled=True)
    model_field, lines = pl.pallas_call(
        lines_kernel,
        out_shape=(shape((64, NY), BF16), shape((N_PENCIL, CHUNK, 128), BF16)),
        in_specs=[pl.BlockSpec(memory_space=pltpu.SMEM)] + [pl.BlockSpec(memory_space=pltpu.VMEM)] * 5,
        scratch_shapes=[pltpu.VMEM((CH, 256, 256), BF16), pltpu.VMEM((CH, 64, NY), F32)],
        compiler_params=params(),
    )(bias_values, lines, k_row, k_rim, observed[0], precision[0])
    lines = lax.all_to_all(lines, "pencil", split_axis=0, concat_axis=0, tiled=True)
    field = call(
        adjoint_kernel,
        shape((2112, 128), BF16),
        [pltpu.VMEM((CH, NZ, 128), BF16), pltpu.VMEM((CH, NZ, 128), F32)],
    )(lines, k_col)
    field_up = lax.ppermute(field, "slab", forth)
    field_dn = lax.ppermute(field, "slab", aft)
    sampled = call(
        sample_kernel,
        shape((TILES, GRADS), BF16),
        [
            pltpu.VMEM((CH, 1056, 256), BF16),
            pltpu.VMEM((256, 1536), BF16),
            pltpu.VMEM((72, 512), F32),
            pltpu.VMEM((GRADS, TILES), F32),
        ],
    )(turned, field, field_up, field_dn)
    came_back = lax.all_to_all(sampled, both, split_axis=0, concat_axis=0, tiled=True)
    grads = call(unpack_kernel, shape((7, 128, 128), F32), [pltpu.VMEM((TILES, 128), F32)])(
        came_back, table
    )
    return (grads.reshape(7, PART_DEV), model_field[None])


def solution(mesh):
    return jax.shard_map(
        per_device,
        mesh=mesh,
        in_specs=(
            P(None, ("slab", "pencil")),
            P(None, ("slab", "pencil")),
            P(None, ("slab", "pencil")),
            P(("slab", "pencil"), None, None),
            P(),
            P(),
            P("slab", "pencil", None),
            P("slab", "pencil", None),
        ),
        out_specs=(P(None, ("slab", "pencil")), P("slab", "pencil", None)),
        check_vma=False,
    )
```

```python
import jax
import jax.numpy as jnp
from jax import lax
from jax.experimental import pallas as pl
from jax.experimental.pallas import tpu as pltpu
from jax.sharding import PartitionSpec as P

NY = 1024
NZ = 1024
ZB = 32
PART_DEV = 16384
TILES = 256
CAP = 2
TY = 64
LANES = 64
RECORD = 12 * LANES
GRADS = 7 * LANES
CH = 4
N_PENCIL = 16
CHUNK = 136
F32 = jnp.float32
BF16 = jnp.bfloat16

R_GX, R_GY, R_GZ, R_LOW, R_CY, R_CZ = 4, 5, 6, 3, 10, 11


PAIRS = RECORD // 128
BACK = 4


def params(mebibytes):
    return pltpu.CompilerParams(vmem_limit_bytes=mebibytes * 1024 * 1024)


def lanes_of(shape):
    return lax.broadcasted_iota(jnp.int32, shape, len(shape) - 1)


def live_rows(counts_ref, scr):
    lane = lanes_of((ZB, 128))
    block = lax.broadcasted_iota(jnp.int32, (ZB, 128), 0)
    spread = jnp.where((lane % LANES) // CAP == block, 1.0, 0.0).astype(BF16)
    held = lax.dot_general(
        counts_ref[...].astype(F32).astype(BF16),
        spread,
        (((0,), (0,)), ((), ())),
        preferred_element_type=F32,
    )
    rank = (lanes_of((TILES, 128)) % CAP).astype(F32)
    scr[0:TILES] = jnp.where(rank < held, 1.0, 0.0)
    return scr[pl.ds(0, 128, stride=2), :] > 0.0, scr[pl.ds(1, 128, stride=2), :] > 0.0


def pack_kernel(fr_ref, ci_ref, wt_ref, cn_ref, out_ref, scr, mask):
    low = lanes_of((128, 128)) < LANES
    live = live_rows(cn_ref, mask)

    def put(k, a, b, masked=False):
        even = jnp.where(low, a, pltpu.roll(b, LANES, 1))
        odd = jnp.where(low, pltpu.roll(a, LANES, 1), b)
        if masked:
            even, odd = jnp.where(live[0], even, 0.0), jnp.where(live[1], odd, 0.0)
        scr[pl.ds(k, 128, stride=2 * PAIRS), :] = even
        scr[pl.ds(PAIRS + k, 128, stride=2 * PAIRS), :] = odd

    weights = wt_ref[...].astype(F32)
    put(0, weights[:, 0, :], weights[:, 1, :], True)
    put(1, weights[:, 2, :], weights[:, 3, :], True)
    offsets = [fr_ref[:, d, :] - 0.5 for d in range(3)]
    high = [g.astype(BF16).astype(F32) for g in offsets]
    rest = [g - h for g, h in zip(offsets, high)]
    put(2, high[0], high[1])
    put(3, high[2], rest[0])
    put(4, rest[1], rest[2])
    put(5, ci_ref[:, 1, :].astype(F32), ci_ref[:, 2, :].astype(F32))
    out_ref[...] = scr[0 : TILES * PAIRS].astype(BF16)


def unpack_kernel(in_ref, cn_ref, out_ref, scr, mask):
    low = lanes_of((128, 128)) < LANES
    live = live_rows(cn_ref, mask)
    scr[0 : TILES * BACK] = in_ref[...].astype(F32)
    for j in range(BACK):
        even = jnp.where(live[0], scr[pl.ds(j, 128, stride=2 * BACK), :], 0.0)
        odd = jnp.where(live[1], scr[pl.ds(BACK + j, 128, stride=2 * BACK), :], 0.0)
        out_ref[:, 2 * j, :] = jnp.where(low, even, pltpu.roll(odd, LANES, 1))
        if j < 3:
            out_ref[:, 2 * j + 1, :] = jnp.where(low, pltpu.roll(even, LANES, 1), odd)


def transpose_records(x_ref, wide, xt_ref):
    wide[0 : TILES * PAIRS] = x_ref[...].astype(F32)
    for k in range(PAIRS):
        for h in range(2):
            piece = wide[pl.ds(h * 128 * PAIRS + k, 128, stride=PAIRS), :]
            xt_ref[k * 128 : k * 128 + 128, h * 128 : h * 128 + 128] = piece.T
    first, last = R_GX * LANES, R_GZ * LANES + LANES
    xt_ref[first:last, :] += xt_ref[first + R_LOW * LANES : last + R_LOW * LANES, :]


def slot_row(xt_ref, r, b):
    first = xt_ref[pl.ds(r * LANES + 2 * b, 1), :]
    second = xt_ref[pl.ds(r * LANES + 2 * b + 1, 1), :]
    return jnp.concatenate([first, second], axis=1)


def hat(places, centre):
    return jnp.maximum(1.0 - jnp.abs(places - centre), 0.0)


def rim_places(rows):
    row = lax.broadcasted_iota(jnp.int32, (rows, 128), 0)
    y = jnp.where(row == 64, -1, jnp.where(row == 65, 64, jnp.where(row > 65, 1000, row)))
    return y.astype(F32)


def deposit(xt_ref, acc_ref, yv_ref, zv_ref, side):
    def block(b, carry):
        gx = slot_row(xt_ref, R_GX, b)
        if side == 0:
            wx = 1.0 - jnp.abs(gx)
        elif side < 0:
            wx = jnp.maximum(-gx, 0.0)
        else:
            wx = jnp.maximum(gx, 0.0)
        py = slot_row(xt_ref, R_CY, b) + slot_row(xt_ref, R_GY, b)
        pz = slot_row(xt_ref, R_CZ, b) + slot_row(xt_ref, R_GZ, b) + 1.0
        plane = (wx * hat(yv_ref[...], py)).astype(BF16)
        wz = hat(zv_ref[...], pz)
        column = jnp.concatenate([slot_row(xt_ref, c, b) * wz for c in range(CH)], axis=0).astype(BF16)
        add = lax.dot_general(column, plane, (((1,), (1,)), ((), ())), preferred_element_type=F32)
        at = pl.multiple_of(b * ZB, ZB)
        for c in range(CH):
            acc_ref[c, pl.ds(at, 40), 0:72] += add[c * 40 : c * 40 + 40]
        return carry

    lax.fori_loop(0, NZ // ZB, block, 0, unroll=4)


def fill_places(yv_ref, zv_ref):
    yv = rim_places(72)
    zv = lax.broadcasted_iota(jnp.int32, (40, 128), 0).astype(F32)
    for k in range(4):
        yv_ref[:, k * 128 : k * 128 + 128] = yv
        zv_ref[:, k * 128 : k * 128 + 128] = zv


def own_kernel(x_ref, acc_ref, xt_ref, wide, yv_ref, zv_ref):
    fill_places(yv_ref, zv_ref)
    transpose_records(x_ref, wide, xt_ref)
    acc_ref[...] = jnp.zeros_like(acc_ref)
    deposit(xt_ref, acc_ref, yv_ref, zv_ref, 0)


def along_z(field_ref, col_ref, out_ref):
    def channel(c, carry):
        for half in range(2):
            pair = jnp.concatenate(
                [
                    field_ref[c, (2 * half) * 256 : (2 * half) * 256 + 256, :],
                    field_ref[c, (2 * half + 1) * 256 : (2 * half + 1) * 256 + 256, :],
                ],
                axis=1,
            )
            prods = [
                jnp.dot(col_ref[c, d * 256 : d * 256 + 256, :], pair, preferred_element_type=F32)
                for d in range(4)
            ]
            for j in range(4):
                part = prods[(j - 2 * half) % 4][:, 0:128] + prods[(j - 2 * half - 1) % 4][:, 128:256]
                if half == 0:
                    out_ref[c, j * 256 : j * 256 + 256, :] = part
                else:
                    out_ref[c, j * 256 : j * 256 + 256, :] += part
        return carry

    lax.fori_loop(0, CH, channel, 0)


def rim_rows(parts, rows):
    lane = lanes_of((rows, 128))
    table = jnp.zeros((rows, 128), F32)
    for c in range(CH):
        table = jnp.where(lane // 2 == c, pltpu.roll(parts[c], LANES + 2 * c, 1), table)
    return table.T[0:8]


def forward_kernel(up_ref, dn_ref, start_ref, col_ref, out_ref, acc, xt, wide, yv, zv, dens, smooth):
    fill_places(yv, zv)
    acc[...] = start_ref[...]
    transpose_records(up_ref, wide, xt)
    deposit(xt, acc, yv, zv, 1)
    transpose_records(dn_ref, wide, xt)
    deposit(xt, acc, yv, zv, -1)
    acc[:, NZ : NZ + 1, :] += acc[:, 0:1, :]
    acc[:, 1:2, :] += acc[:, NZ + 1 : NZ + 2, :]
    dens[...] = acc[:, 1 : NZ + 1, :].astype(BF16)
    along_z(dens, col_ref, smooth)
    low = lanes_of((64, 128)) < LANES

    def send(p, carry):
        at = pl.multiple_of(p * 64, 64)
        parts = [smooth[c, pl.ds(at, 64), :] for c in range(CH)]
        for pair in range(2):
            both = jnp.where(low, parts[2 * pair], pltpu.roll(parts[2 * pair + 1], LANES, 1))
            out_ref[p, pair * 64 : pair * 64 + 64, :] = both.astype(BF16)
        rims = rim_rows(parts, 64)
        out_ref[p, 128:136, :] = jnp.concatenate([rims, jnp.zeros((8, 64), F32)], axis=1).astype(BF16)
        return carry

    lax.fori_loop(0, N_PENCIL, send, 0)


def wrapped_sum(prod):
    blocks = []
    for j in range(4):
        total = prod[0:64, j * 256 : j * 256 + 256]
        for i in range(1, 4):
            d = (j - i) % 4
            total = total + prod[i * 64 : i * 64 + 64, d * 256 : d * 256 + 256]
        blocks.append(total)
    return jnp.concatenate(blocks, axis=1)


def lines_kernel(bias_ref, in_ref, row_ref, rim_ref, obs_ref, prec_ref, model_ref, out_ref, left, back):
    low = lanes_of((64, 128)) < LANES
    for pair in range(2):
        for pp in range(8):
            a = in_ref[2 * pp, pair * 64 : pair * 64 + 64, :].astype(F32)
            b = in_ref[2 * pp + 1, pair * 64 : pair * 64 + 64, :].astype(F32)
            i, at = pp // 2, (pp % 2) * 128
            left[2 * pair, i * 64 : i * 64 + 64, at : at + 128] = jnp.where(
                low, a, pltpu.roll(b, LANES, 1)
            ).astype(BF16)
            left[2 * pair + 1, i * 64 : i * 64 + 64, at : at + 128] = jnp.where(
                low, pltpu.roll(a, LANES, 1), b
            ).astype(BF16)
    which = lax.broadcasted_iota(jnp.int32, (128, 64), 0) % 8 // 2
    bias = jnp.zeros((128, 64), F32)
    for c in range(CH):
        bias = jnp.where(which == c, bias_ref[c], bias)
    rims = jnp.concatenate([in_ref[p, 128:136, 0:64].astype(F32) for p in range(N_PENCIL)], axis=0)
    rims = (rims * bias).T.astype(BF16)
    model = jnp.dot(rims, rim_ref[...], preferred_element_type=F32)
    for c in range(CH):
        prod = jnp.dot(left[c], row_ref[c], preferred_element_type=F32)
        model = model + bias_ref[c] * wrapped_sum(prod)
    model_ref[...] = model.astype(BF16)
    pull = (prec_ref[...] * (model - obs_ref[...])).astype(BF16)
    stacked = jnp.concatenate([pull[:, i * 256 : i * 256 + 256] for i in range(4)], axis=0)
    for c in range(CH):
        prod = jnp.dot(stacked, row_ref[c], preferred_element_type=F32)
        back[c] = bias_ref[c] * wrapped_sum(prod)
    for pair in range(2):
        for pp in range(8):
            a = back[2 * pair, :, pp * 128 : pp * 128 + 128]
            b = back[2 * pair + 1, :, pp * 128 : pp * 128 + 128]
            out_ref[2 * pp, pair * 64 : pair * 64 + 64, :] = jnp.where(
                low, a, pltpu.roll(b, LANES, 1)
            ).astype(BF16)
            out_ref[2 * pp + 1, pair * 64 : pair * 64 + 64, :] = jnp.where(
                low, pltpu.roll(a, LANES, 1), b
            ).astype(BF16)
    rims = lax.dot_general(rim_ref[...], pull, (((1,), (1,)), ((), ())), preferred_element_type=F32)
    rims = jnp.concatenate([rims * bias, jnp.zeros((128, 64), F32)], axis=1).astype(BF16)
    for p in range(N_PENCIL):
        out_ref[p, 128:136, :] = rims[p * 8 : p * 8 + 8]


def adjoint_kernel(in_ref, col_ref, out_ref, field, smooth):
    lane = lanes_of((64, 128))
    low = lane < LANES

    def take(p, carry):
        at = pl.multiple_of(p * 64, 64)
        rims = in_ref[p, 128:136, :].astype(F32)
        table = jnp.concatenate([rims, jnp.zeros((120, 128), F32)], axis=0).T[0:64]
        for pair in range(2):
            both = in_ref[p, pair * 64 : pair * 64 + 64, :].astype(F32)
            for k in range(2):
                c = 2 * pair + k
                main = both if k == 0 else pltpu.roll(both, LANES, 1)
                rim = jnp.where(lane < 66, pltpu.roll(table, LANES - 2 * c, 1), 0.0)
                field[c, pl.ds(at, 64), :] = jnp.where(low, main, rim).astype(BF16)
        return carry

    lax.fori_loop(0, N_PENCIL, take, 0)
    along_z(field, col_ref, smooth)
    wide = lanes_of((128, 128)) < LANES
    for q in range(8):
        parts = [smooth[c, q * 128 : q * 128 + 128, :] for c in range(CH)]
        for pair in range(2):
            both = jnp.where(wide, parts[2 * pair], pltpu.roll(parts[2 * pair + 1], LANES, 1))
            out_ref[pair * 1024 + q * 128 : pair * 1024 + q * 128 + 128, :] = both.astype(BF16)
        out_ref[2048 + q * 8 : 2048 + q * 8 + 8, :] = rim_rows(parts, 128).astype(BF16)


def sample_kernel(xt_ref, own_ref, up_ref, dn_ref, out_ref, field, planes, yv, ot, tall):
    lane = lanes_of((128, 128))
    low = lane < LANES

    def fill(q, carry):
        at = pl.multiple_of(q * 128, 128)
        to = pl.multiple_of(q * 128 + 16, 16)
        rim_at = pl.multiple_of(2048 + q * 8, 8)
        tables = []
        for ref in (own_ref, up_ref, dn_ref):
            rims = ref[pl.ds(rim_at, 8), :].astype(F32)
            tables.append(jnp.concatenate([rims, jnp.zeros((120, 128), F32)], axis=0).T)
        for pair in range(2):
            own = own_ref[pl.ds(pair * 1024 + at, 128), :].astype(F32)
            up = up_ref[pl.ds(pair * 1024 + at, 128), :].astype(F32)
            dn = dn_ref[pl.ds(pair * 1024 + at, 128), :].astype(F32)
            for k in range(2):
                c = 2 * pair + k
                if k == 0:
                    first = jnp.where(low, up, pltpu.roll(dn, LANES, 1))
                    main = own
                else:
                    first = jnp.where(low, pltpu.roll(up, LANES, 1), dn)
                    main = pltpu.roll(own, LANES, 1)
                rim = jnp.zeros((128, 128), F32)
                for s in range(3):
                    here = pltpu.roll(tables[s], LANES + 2 * s - 2 * c, 1)
                    rim = jnp.where((lane - LANES) // 2 == s, here, rim)
                field[c, pl.ds(to, 128), 0:128] = first.astype(BF16)
                field[c, pl.ds(to, 128), 128:256] = jnp.where(low, main, rim).astype(BF16)
        return carry

    lax.fori_loop(0, 8, fill, 0)
    field[:, 0:16, :] = field[:, 1024:1040, :]
    field[:, 1040:1056, :] = field[:, 16:32, :]
    planes[...] = jnp.zeros_like(planes)
    row = lax.broadcasted_iota(jnp.int32, (72, 512), 0)
    yv[...] = jnp.where(row < 64, row, jnp.where(row % 2 == 0, -1, 64)).astype(F32)
    zv = (lax.broadcasted_iota(jnp.int32, (48, 512), 0) + 8).astype(F32)
    part = lax.broadcasted_iota(jnp.int32, (8, 512), 0) // 2

    def block(b, carry):
        gx, gy, gz = (slot_row(xt_ref, r, b) for r in (R_GX, R_GY, R_GZ))
        cy, cz = slot_row(xt_ref, R_CY, b), slot_row(xt_ref, R_CZ, b)
        fall_x, fall_y, fall_z = gx < 0.0, gy < 0.0, gz < 0.0
        wx = [jnp.maximum(-gx, 0.0), jnp.maximum(gx, 0.0), 1.0 - jnp.abs(gx)]
        sx = [jnp.where(fall_x, -1.0, 0.0), jnp.where(fall_x, 0.0, 1.0), jnp.where(fall_x, 1.0, -1.0)]
        places = yv[...]
        wy = hat(places, cy + gy)
        step_y = places - jnp.where(fall_y, cy - 1.0, cy)
        sy = jnp.where(step_y == 0.0, -1.0, jnp.where(step_y == 1.0, 1.0, 0.0))
        wx16, sx16 = ([a.astype(BF16) for a in ax] for ax in (wx, sx))
        wy16, sy16 = wy[0:64].astype(BF16), sy[0:64].astype(BF16)
        for s in range(3):
            rows = slice(s * 64, s * 64 + 64)
            planes[rows, 0:512] = (wx[s] * wy[0:64]).astype(BF16)
            planes[rows, 512:1024] = sx16[s] * wy16
            planes[rows, 1024:1536] = wx16[s] * sy16
        for k, (ax, ay) in enumerate(((wx, wy), (sx, wy), (wx, sy))):
            rim = jnp.where(
                part == 0, ax[2], jnp.where(part == 1, ax[0], jnp.where(part == 2, ax[1], 0.0))
            )
            rim = jnp.concatenate([rim * ay[64:72], jnp.zeros((8, 512), F32)], axis=0)
            planes[192:208, k * 512 : k * 512 + 512] = rim.astype(BF16)
        at = pl.multiple_of(b * ZB, ZB)
        here = jnp.concatenate([field[c, pl.ds(at, 64), :] for c in range(CH)], axis=0)
        wz = hat(zv, cz + gz + 16.0)
        step_z = zv - jnp.where(fall_z, cz + 15.0, cz + 16.0)
        sz = jnp.where(step_z == 0.0, -1.0, jnp.where(step_z == 1.0, 1.0, 0.0))
        masses = [slot_row(xt_ref, c, b) for c in range(CH)]
        values = jnp.dot(here, planes[:, 0:512], preferred_element_type=F32)
        grads = []
        slope_z = jnp.zeros((1, 512), F32)
        for c in range(CH):
            v = values[c * 64 + 8 : c * 64 + 56]
            grads.append(jnp.sum(v * wz, axis=0, keepdims=True))
            slope_z = slope_z + masses[c] * jnp.sum(v * sz, axis=0, keepdims=True)
        for k in (1, 2):
            slopes = jnp.dot(here, planes[:, k * 512 : k * 512 + 512], preferred_element_type=F32)
            total = jnp.zeros((48, 512), F32)
            for c in range(CH):
                total = total + masses[c] * slopes[c * 64 + 8 : c * 64 + 56]
            grads.append(jnp.sum(total * wz, axis=0, keepdims=True))
        grads.append(slope_z)
        for r in range(7):
            ot[pl.ds(r * LANES + 2 * b, 1), :] = grads[r][:, 0:256]
            ot[pl.ds(r * LANES + 2 * b + 1, 1), :] = grads[r][:, 256:512]
        return carry

    lax.fori_loop(0, NZ // ZB, block, 0, unroll=2)
    ot[GRADS:, :] = jnp.zeros((LANES, TILES), F32)
    for j in range(BACK):
        for h in range(2):
            piece = ot[j * 128 : j * 128 + 128, h * 128 : h * 128 + 128]
            tall[pl.ds(h * 128 * BACK + j, 128, stride=BACK), :] = piece.T
    out_ref[...] = tall[0 : TILES * BACK].astype(BF16)


def correlation(smoothing, rows, columns):
    distance = jnp.abs(rows - columns)
    distance = jnp.minimum(distance, NY - distance).astype(F32)
    breadth = smoothing
    profile = jnp.exp(-distance * distance / (2.0 * breadth * breadth)) / jnp.sqrt(breadth)
    return (profile + jnp.where(distance == 0.0, 1.0, 0.0)).astype(BF16)


def call(kernel, outs, scratch, mebibytes):
    return pl.pallas_call(
        kernel,
        out_shape=outs,
        scratch_shapes=scratch,
        compiler_params=params(mebibytes),
    )


def exchange(rows, wide, axes):
    rows = rows.reshape(TILES, wide, 2, 128).transpose(0, 2, 1, 3).reshape(TILES, 2, wide * 128)
    rows = lax.all_to_all(rows, axes, split_axis=0, concat_axis=0, tiled=True)
    rows = rows.reshape(TILES, 2, wide, 128).transpose(0, 2, 1, 3)
    return rows.reshape(TILES * 2 * wide, 128)


def shape(dims, kind):
    return jax.ShapeDtypeStruct(dims, kind)


def per_device(fractions, cell_index, weights, counts, smoothing, bias_values, observed, precision):
    both = ("slab", "pencil")
    count = lax.axis_size("slab")
    forth = [(i, (i + 1) % count) for i in range(count)]
    aft = [((i + 1) % count, i) for i in range(count)]

    ids = jnp.arange(NY, dtype=jnp.int32)
    breadth = smoothing[:, None, None]
    k_row = correlation(breadth, ids[None, :256, None], ids[None, None, :])
    k_col = correlation(breadth, ids[None, :, None], ids[None, None, :256])
    rim = jnp.arange(128, dtype=jnp.int32)
    rim_y = (rim // 8 * TY - 1 + rim % 2 * (TY + 1)) % NY
    k_rim = correlation(smoothing[rim % 8 // 2][:, None], rim_y[:, None], ids[None, :])

    table = counts[0].T
    split = [a.reshape(a.shape[0], 128, 128).transpose(1, 0, 2) for a in (fractions, cell_index, weights)]
    mask = pltpu.VMEM((TILES + 8, 128), F32)
    records = call(
        pack_kernel,
        shape((TILES * PAIRS, 128), BF16),
        [pltpu.VMEM((TILES * PAIRS + 16, 128), F32), mask],
        12,
    )(*split, table)
    arrived = exchange(records, PAIRS // 2, both)
    arrived, k_row, k_col, k_rim = lax.optimization_barrier((arrived, k_row, k_col, k_rim))
    from_up = lax.ppermute(arrived, "slab", forth)
    from_dn = lax.ppermute(arrived, "slab", aft)
    turned = pltpu.VMEM((RECORD, TILES), F32)
    wide = pltpu.VMEM((TILES * PAIRS + 8, 128), F32)
    places = [pltpu.VMEM((72, 512), F32), pltpu.VMEM((40, 512), F32)]
    acc, xt = call(
        own_kernel,
        (shape((CH, 1040, 128), F32), shape((RECORD, TILES), F32)),
        [wide] + places,
        12,
    )(arrived)
    lines = call(
        forward_kernel,
        shape((N_PENCIL, CHUNK, 128), BF16),
        [pltpu.VMEM((CH, 1040, 128), F32), turned, wide]
        + places
        + [pltpu.VMEM((CH, NZ, 128), BF16), pltpu.VMEM((CH, NZ, 128), F32)],
        24,
    )(from_up, from_dn, acc, k_col)
    lines = lax.all_to_all(lines, "pencil", split_axis=0, concat_axis=0, tiled=True)
    model_field, lines = pl.pallas_call(
        lines_kernel,
        out_shape=(shape((64, NY), BF16), shape((N_PENCIL, CHUNK, 128), BF16)),
        in_specs=[pl.BlockSpec(memory_space=pltpu.SMEM)] + [pl.BlockSpec(memory_space=pltpu.VMEM)] * 5,
        scratch_shapes=[pltpu.VMEM((CH, 256, 256), BF16), pltpu.VMEM((CH, 64, NY), F32)],
        compiler_params=params(20),
    )(bias_values, lines, k_row, k_rim, observed[0], precision[0])
    lines = lax.all_to_all(lines, "pencil", split_axis=0, concat_axis=0, tiled=True)
    field = call(
        adjoint_kernel,
        shape((2112, 128), BF16),
        [pltpu.VMEM((CH, NZ, 128), BF16), pltpu.VMEM((CH, NZ, 128), F32)],
        20,
    )(lines, k_col)
    field_up = lax.ppermute(field, "slab", forth)
    field_dn = lax.ppermute(field, "slab", aft)
    sampled = call(
        sample_kernel,
        shape((TILES * BACK, 128), BF16),
        [
            pltpu.VMEM((CH, 1056, 256), BF16),
            pltpu.VMEM((256, 1536), BF16),
            pltpu.VMEM((72, 512), F32),
            pltpu.VMEM((BACK * 128, TILES), F32),
            pltpu.VMEM((TILES * BACK + 8, 128), F32),
        ],
        20,
    )(xt, field, field_up, field_dn)
    came_back = lax.all_to_all(
        sampled.reshape(TILES, BACK, 128), both, split_axis=0, concat_axis=0, tiled=True
    ).reshape(TILES * BACK, 128)
    grads = call(
        unpack_kernel,
        shape((128, 7, 128), F32),
        [pltpu.VMEM((TILES * BACK + 8, 128), F32), mask],
        12,
    )(came_back, table)
    return (grads.transpose(1, 0, 2).reshape(7, PART_DEV), model_field[None])


def solution(mesh):
    return jax.shard_map(
        per_device,
        mesh=mesh,
        in_specs=(
            P(None, ("slab", "pencil")),
            P(None, ("slab", "pencil")),
            P(None, ("slab", "pencil")),
            P(("slab", "pencil"), None, None),
            P(),
            P(),
            P("slab", "pencil", None),
            P("slab", "pencil", None),
        ),
        out_specs=(P(None, ("slab", "pencil")), P("slab", "pencil", None)),
        check_vma=False,
    )
```

```python
import functools

import jax
import jax.numpy as jnp
from jax import lax
from jax.experimental import pallas as pl
from jax.experimental.pallas import tpu as pltpu
from jax.sharding import PartitionSpec as P

NY = 1024
NZ = 1024
ZB = 32
PART_DEV = 16384
TILES = 256
CAP = 2
TY = 64
LANES = 64
RECORD = 12 * LANES
GRADS = 7 * LANES
CH = 4
N_PENCIL = 16
CHUNK = 136
F32 = jnp.float32
BF16 = jnp.bfloat16

R_GX, R_GY, R_GZ, R_LOW, R_CY, R_CZ = 4, 5, 6, 3, 10, 11


PAIRS = RECORD // 128
BACK = 4


def params(mebibytes):
    return pltpu.CompilerParams(vmem_limit_bytes=mebibytes * 1024 * 1024)


def lanes_of(shape):
    return lax.broadcasted_iota(jnp.int32, shape, len(shape) - 1)


def live_rows(counts_ref, scr):
    lane = lanes_of((ZB, 128))
    block = lax.broadcasted_iota(jnp.int32, (ZB, 128), 0)
    spread = jnp.where((lane % LANES) // CAP == block, 1.0, 0.0).astype(BF16)
    held = lax.dot_general(
        counts_ref[...].astype(F32).astype(BF16),
        spread,
        (((0,), (0,)), ((), ())),
        preferred_element_type=F32,
    )
    rank = (lanes_of((TILES, 128)) % CAP).astype(F32)
    scr[0:TILES] = jnp.where(rank < held, 1.0, 0.0)
    return scr[pl.ds(0, 128, stride=2), :] > 0.0, scr[pl.ds(1, 128, stride=2), :] > 0.0


def pack_kernel(fr_ref, ci_ref, wt_ref, cn_ref, out_ref, scr, mask):
    low = lanes_of((128, 128)) < LANES
    live = live_rows(cn_ref, mask)

    def put(k, a, b, masked=False):
        even = jnp.where(low, a, pltpu.roll(b, LANES, 1))
        odd = jnp.where(low, pltpu.roll(a, LANES, 1), b)
        if masked:
            even, odd = jnp.where(live[0], even, 0.0), jnp.where(live[1], odd, 0.0)
        scr[pl.ds(k, 128, stride=2 * PAIRS), :] = even
        scr[pl.ds(PAIRS + k, 128, stride=2 * PAIRS), :] = odd

    weights = wt_ref[...].astype(F32)
    put(0, weights[:, 0, :], weights[:, 1, :], True)
    put(1, weights[:, 2, :], weights[:, 3, :], True)
    offsets = [fr_ref[:, d, :] - 0.5 for d in range(3)]
    high = [g.astype(BF16).astype(F32) for g in offsets]
    rest = [g - h for g, h in zip(offsets, high)]
    put(2, high[0], high[1])
    put(3, high[2], rest[0])
    put(4, rest[1], rest[2])
    put(5, ci_ref[:, 1, :].astype(F32), ci_ref[:, 2, :].astype(F32))
    out_ref[...] = scr[0 : TILES * PAIRS].astype(BF16)


def unpack_kernel(in_ref, cn_ref, out_ref, scr, mask):
    low = lanes_of((128, 128)) < LANES
    live = live_rows(cn_ref, mask)
    scr[0 : TILES * BACK] = in_ref[...].astype(F32)
    for j in range(BACK):
        even = jnp.where(live[0], scr[pl.ds(j, 128, stride=2 * BACK), :], 0.0)
        odd = jnp.where(live[1], scr[pl.ds(BACK + j, 128, stride=2 * BACK), :], 0.0)
        out_ref[:, 2 * j, :] = jnp.where(low, even, pltpu.roll(odd, LANES, 1))
        if j < 3:
            out_ref[:, 2 * j + 1, :] = jnp.where(low, pltpu.roll(even, LANES, 1), odd)


def transpose_records(x_ref, wide, xt_ref):
    wide[0 : TILES * PAIRS] = x_ref[...].astype(F32)
    for k in range(PAIRS):
        for h in range(2):
            piece = wide[pl.ds(h * 128 * PAIRS + k, 128, stride=PAIRS), :]
            xt_ref[k * 128 : k * 128 + 128, h * 128 : h * 128 + 128] = piece.T
    first, last = R_GX * LANES, R_GZ * LANES + LANES
    xt_ref[first:last, :] += xt_ref[first + R_LOW * LANES : last + R_LOW * LANES, :]


def slot_row(xt_ref, r, b):
    first = xt_ref[pl.ds(r * LANES + 2 * b, 1), :]
    second = xt_ref[pl.ds(r * LANES + 2 * b + 1, 1), :]
    return jnp.concatenate([first, second], axis=1)


def hat(places, centre):
    return jnp.maximum(1.0 - jnp.abs(places - centre), 0.0)


def rim_places(rows):
    row = lax.broadcasted_iota(jnp.int32, (rows, 128), 0)
    y = jnp.where(row == 64, -1, jnp.where(row == 65, 64, jnp.where(row > 65, 1000, row)))
    return y.astype(F32)


def deposit(xt_ref, acc_ref, yv_ref, zv_ref, side):
    def block(b, carry):
        gx = slot_row(xt_ref, R_GX, b)
        if side == 0:
            wx = 1.0 - jnp.abs(gx)
        elif side < 0:
            wx = jnp.maximum(-gx, 0.0)
        else:
            wx = jnp.maximum(gx, 0.0)
        py = slot_row(xt_ref, R_CY, b) + slot_row(xt_ref, R_GY, b)
        pz = slot_row(xt_ref, R_CZ, b) + slot_row(xt_ref, R_GZ, b) + 1.0
        plane = (wx * hat(yv_ref[...], py)).astype(BF16)
        wz = hat(zv_ref[...], pz)
        column = jnp.concatenate([slot_row(xt_ref, c, b) * wz for c in range(CH)], axis=0).astype(BF16)
        add = lax.dot_general(column, plane, (((1,), (1,)), ((), ())), preferred_element_type=F32)
        at = pl.multiple_of(b * ZB, ZB)
        for c in range(CH):
            acc_ref[c, pl.ds(at, 40), 0:72] += add[c * 40 : c * 40 + 40]
        return carry

    lax.fori_loop(0, NZ // ZB, block, 0, unroll=16)


def fill_places(yv_ref, zv_ref):
    yv = rim_places(72)
    zv = lax.broadcasted_iota(jnp.int32, (40, 128), 0).astype(F32)
    for k in range(4):
        yv_ref[:, k * 128 : k * 128 + 128] = yv
        zv_ref[:, k * 128 : k * 128 + 128] = zv


def own_kernel(x_ref, acc_ref, xt_ref, wide, yv_ref, zv_ref):
    fill_places(yv_ref, zv_ref)
    transpose_records(x_ref, wide, xt_ref)
    acc_ref[...] = jnp.zeros_like(acc_ref)
    deposit(xt_ref, acc_ref, yv_ref, zv_ref, 0)


def along_z(field_ref, col_ref, out_ref, first, count):
    def channel(c, carry):
        quarters = [field_ref[c, i * 256 : i * 256 + 256, :] for i in range(4)]
        pairs = [jnp.concatenate(quarters[i : i + 2], axis=1) for i in (0, 2)]
        right = jnp.concatenate(pairs, axis=0)
        cols = [col_ref[first + c, d * 256 : d * 256 + 256, :] for d in range(4)]
        prods = [
            jnp.dot(
                jnp.concatenate([cols[d], cols[(d - 2) % 4]], axis=1),
                right,
                preferred_element_type=F32,
            )
            for d in range(4)
        ]
        for j in range(4):
            out_ref[c, j * 256 : j * 256 + 256, :] = prods[j][:, 0:128] + prods[(j - 1) % 4][:, 128:256]
        return carry

    lax.fori_loop(0, count, channel, 0, unroll=2)


def rim_rows(parts, rows):
    lane = lanes_of((rows, 128))
    table = jnp.zeros((rows, 128), F32)
    for c, part in enumerate(parts):
        table = jnp.where(lane // 2 == c, pltpu.roll(part, LANES + 2 * c, 1), table)
    return table.T[0:8]


def forward_kernel(up_ref, dn_ref, start_ref, col_ref, out_ref, acc, xt, wide, yv, zv, dens, smooth):
    fill_places(yv, zv)
    acc[...] = start_ref[...]
    transpose_records(up_ref, wide, xt)
    deposit(xt, acc, yv, zv, 1)
    transpose_records(dn_ref, wide, xt)
    deposit(xt, acc, yv, zv, -1)
    acc[:, NZ : NZ + 1, :] += acc[:, 0:1, :]
    acc[:, 1:2, :] += acc[:, NZ + 1 : NZ + 2, :]
    dens[...] = acc[:, 1 : NZ + 1, :].astype(BF16)
    along_z(dens, col_ref, smooth, 0, CH)
    low = lanes_of((64, 128)) < LANES

    def send(p, carry):
        at = pl.multiple_of(p * 64, 64)
        parts = [smooth[c, pl.ds(at, 64), :] for c in range(CH)]
        for pair in range(2):
            both = jnp.where(low, parts[2 * pair], pltpu.roll(parts[2 * pair + 1], LANES, 1))
            out_ref[p, pair * 64 : pair * 64 + 64, :] = both.astype(BF16)
        rims = rim_rows(parts, 64)
        out_ref[p, 128:136, :] = jnp.concatenate([rims, jnp.zeros((8, 64), F32)], axis=1).astype(BF16)
        return carry

    lax.fori_loop(0, N_PENCIL, send, 0, unroll=16)


def wrapped_sum(prod):
    blocks = []
    for j in range(4):
        total = prod[0:64, j * 256 : j * 256 + 256]
        for i in range(1, 4):
            d = (j - i) % 4
            total = total + prod[i * 64 : i * 64 + 64, d * 256 : d * 256 + 256]
        blocks.append(total)
    return jnp.concatenate(blocks, axis=1)


def lines_kernel(bias_ref, in_ref, row_ref, rim_ref, obs_ref, prec_ref, model_ref, out_ref, left, back):
    low = lanes_of((64, 128)) < LANES
    for pair in range(2):
        for pp in range(8):
            a = in_ref[2 * pp, pair * 64 : pair * 64 + 64, :].astype(F32)
            b = in_ref[2 * pp + 1, pair * 64 : pair * 64 + 64, :].astype(F32)
            i, at = pp // 2, (pp % 2) * 128
            left[2 * pair, i * 64 : i * 64 + 64, at : at + 128] = jnp.where(
                low, a, pltpu.roll(b, LANES, 1)
            ).astype(BF16)
            left[2 * pair + 1, i * 64 : i * 64 + 64, at : at + 128] = jnp.where(
                low, pltpu.roll(a, LANES, 1), b
            ).astype(BF16)
    which = lax.broadcasted_iota(jnp.int32, (128, 64), 0) % 8 // 2
    bias = jnp.zeros((128, 64), F32)
    for c in range(CH):
        bias = jnp.where(which == c, bias_ref[c], bias)
    rims = jnp.concatenate([in_ref[p, 128:136, 0:64].astype(F32) for p in range(N_PENCIL)], axis=0)
    rims = (rims * bias).T.astype(BF16)
    model = jnp.dot(rims, rim_ref[...], preferred_element_type=F32)
    for c in range(CH):
        prod = jnp.dot(left[c], row_ref[c], preferred_element_type=F32)
        model = model + bias_ref[c] * wrapped_sum(prod)
    model_ref[...] = model.astype(BF16)
    pull = (prec_ref[...] * (model - obs_ref[...])).astype(BF16)
    stacked = jnp.concatenate([pull[:, i * 256 : i * 256 + 256] for i in range(4)], axis=0)
    for c in range(CH):
        prod = jnp.dot(stacked, row_ref[c], preferred_element_type=F32)
        back[c] = bias_ref[c] * wrapped_sum(prod)
    for pair in range(2):
        for pp in range(8):
            a = back[2 * pair, :, pp * 128 : pp * 128 + 128]
            b = back[2 * pair + 1, :, pp * 128 : pp * 128 + 128]
            out_ref[2 * pp, pair * 64 : pair * 64 + 64, :] = jnp.where(
                low, a, pltpu.roll(b, LANES, 1)
            ).astype(BF16)
            out_ref[2 * pp + 1, pair * 64 : pair * 64 + 64, :] = jnp.where(
                low, pltpu.roll(a, LANES, 1), b
            ).astype(BF16)
    rims = lax.dot_general(rim_ref[...], pull, (((1,), (1,)), ((), ())), preferred_element_type=F32)
    rims = jnp.concatenate([rims * bias, jnp.zeros((128, 64), F32)], axis=1).astype(BF16)
    for p in range(N_PENCIL):
        out_ref[p, 128:136, :] = rims[p * 8 : p * 8 + 8]


def adjoint_kernel(pair, in_ref, col_ref, out_ref, field, smooth):
    lane = lanes_of((64, 128))
    low = lane < LANES

    def take(p, carry):
        at = pl.multiple_of(p * 64, 64)
        rims = in_ref[p, 128:136, :].astype(F32)
        table = jnp.concatenate([rims, jnp.zeros((120, 128), F32)], axis=0).T[0:64]
        both = in_ref[p, pair * 64 : pair * 64 + 64, :].astype(F32)
        for k in range(2):
            main = both if k == 0 else pltpu.roll(both, LANES, 1)
            rim = jnp.where(lane < 66, pltpu.roll(table, LANES - 2 * (2 * pair + k), 1), 0.0)
            field[k, pl.ds(at, 64), :] = jnp.where(low, main, rim).astype(BF16)
        return carry

    lax.fori_loop(0, N_PENCIL, take, 0, unroll=4)
    along_z(field, col_ref, smooth, 2 * pair, 2)
    wide = lanes_of((128, 128)) < LANES
    for q in range(8):
        parts = [smooth[k, q * 128 : q * 128 + 128, :] for k in range(2)]
        both = jnp.where(wide, parts[0], pltpu.roll(parts[1], LANES, 1))
        out_ref[q * 128 : q * 128 + 128, :] = both.astype(BF16)
        out_ref[NZ + q * 8 : NZ + q * 8 + 8, :] = rim_rows(parts, 128).astype(BF16)


def write_planes(xt_ref, b, places, planes):
    gx, gy, cy = (slot_row(xt_ref, r, b) for r in (R_GX, R_GY, R_CY))
    fall_x, fall_y = gx < 0.0, gy < 0.0
    wx = [jnp.maximum(-gx, 0.0), jnp.maximum(gx, 0.0), 1.0 - jnp.abs(gx)]
    sx = [jnp.where(fall_x, -1.0, 0.0), jnp.where(fall_x, 0.0, 1.0), jnp.where(fall_x, 1.0, -1.0)]
    wy = hat(places, cy + gy)
    step_y = places - jnp.where(fall_y, cy - 1.0, cy)
    sy = jnp.where(step_y == 0.0, -1.0, jnp.where(step_y == 1.0, 1.0, 0.0))
    wx16, sx16 = ([a.astype(BF16) for a in ax] for ax in (wx, sx))
    wy16, sy16 = wy[0:64].astype(BF16), sy[0:64].astype(BF16)
    for s in range(3):
        rows = slice(s * 64, s * 64 + 64)
        planes[rows, 0:512] = (wx[s] * wy[0:64]).astype(BF16)
        planes[rows, 512:1024] = sx16[s] * wy16
        planes[rows, 1024:1536] = wx16[s] * sy16
    part = lax.broadcasted_iota(jnp.int32, (8, 512), 0) // 2
    for k, (ax, ay) in enumerate(((wx, wy), (sx, wy), (wx, sy))):
        rim = jnp.where(
            part == 0, ax[2], jnp.where(part == 1, ax[0], jnp.where(part == 2, ax[1], 0.0))
        )
        rim = jnp.concatenate([rim * ay[64:72], jnp.zeros((8, 512), F32)], axis=0)
        planes[192:208, k * 512 : k * 512 + 512] = rim.astype(BF16)


def fill_field(refs, field):
    lane = lanes_of((128, 128))
    low = lane < LANES

    def fill(q, carry):
        at = pl.multiple_of(q * 128, 128)
        rim_at = pl.multiple_of(NZ + q * 8, 8)
        for pair in range(2):
            tables = []
            for ref in refs[pair]:
                rims = ref[pl.ds(rim_at, 8), :].astype(F32)
                tables.append(jnp.concatenate([rims, jnp.zeros((120, 128), F32)], axis=0).T)
            own, up, dn = (ref[pl.ds(at, 128), :].astype(F32) for ref in refs[pair])
            for k in range(2):
                c = 2 * pair + k
                if k == 0:
                    first = jnp.where(low, up, pltpu.roll(dn, LANES, 1))
                    main = own
                else:
                    first = jnp.where(low, pltpu.roll(up, LANES, 1), dn)
                    main = pltpu.roll(own, LANES, 1)
                rim = jnp.zeros((128, 128), F32)
                for s in range(3):
                    here = pltpu.roll(tables[s], LANES + 2 * s - 2 * k, 1)
                    rim = jnp.where((lane - LANES) // 2 == s, here, rim)
                field[c, pl.ds(at, 128), 0:128] = first.astype(BF16)
                field[c, pl.ds(at, 128), 128:256] = jnp.where(low, main, rim).astype(BF16)
        return carry

    lax.fori_loop(0, 8, fill, 0, unroll=8)
    field[:, NZ : NZ + 16, :] = field[:, 0:16, :]


def sample_kernel(xt_ref, *rest):
    refs, (out_ref, field, planes, yv, ot, tall) = (rest[0:3], rest[3:6]), rest[6:]
    fill_field(refs, field)
    row = lax.broadcasted_iota(jnp.int32, (72, 512), 0)
    yv[...] = jnp.where(row < 64, row, jnp.where(row % 2 == 0, -1, 64)).astype(F32)
    zv = lax.broadcasted_iota(jnp.int32, (40, 512), 0).astype(F32)
    ot[GRADS:, :] = jnp.zeros((LANES, TILES), F32)

    def block(b, table):
        write_planes(xt_ref, b, yv[...], table)
        gz, cz = slot_row(xt_ref, R_GZ, b), slot_row(xt_ref, R_CZ, b)
        at = pl.multiple_of(b * ZB, ZB)
        here = jnp.concatenate([field[c, pl.ds(at, 48), :] for c in range(CH)], axis=0)
        wz = hat(zv, cz + gz + 1.0)
        step_z = zv - jnp.where(gz < 0.0, cz, cz + 1.0)
        sz = jnp.where(step_z == 0.0, -1.0, jnp.where(step_z == 1.0, 1.0, 0.0))
        masses = [slot_row(xt_ref, c, b) for c in range(CH)]
        grads = []
        for k in range(3):
            sampled = jnp.dot(
                here[:, 0:208], table[:, k * 512 : k * 512 + 512], preferred_element_type=F32
            )
            total = jnp.zeros((40, 512), F32)
            for c in range(CH):
                v = sampled[c * 48 : c * 48 + 40]
                if k == 0:
                    grads.append(jnp.sum(v * wz, axis=0, keepdims=True))
                total = total + masses[c] * v
            if k == 0:
                slope_z = jnp.sum(total * sz, axis=0, keepdims=True)
            else:
                grads.append(jnp.sum(total * wz, axis=0, keepdims=True))
        grads.append(slope_z)
        for r in range(7):
            ot[pl.ds(r * LANES + 2 * b, 1), :] = grads[r][:, 0:256]
            ot[pl.ds(r * LANES + 2 * b + 1, 1), :] = grads[r][:, 256:512]

    def two(g, carry):
        block(2 * g, planes.at[0])
        block(2 * g + 1, planes.at[1])
        return carry

    lax.fori_loop(0, NZ // ZB // 2, two, 0)
    for j in range(BACK):
        for h in range(2):
            piece = ot[j * 128 : j * 128 + 128, h * 128 : h * 128 + 128]
            tall[pl.ds(h * 128 * BACK + j, 128, stride=BACK), :] = piece.T
    out_ref[...] = tall[0 : TILES * BACK].astype(BF16)


def correlation(smoothing, rows, columns):
    distance = jnp.abs(rows - columns)
    distance = jnp.minimum(distance, NY - distance).astype(F32)
    breadth = smoothing
    profile = jnp.exp(-distance * distance / (2.0 * breadth * breadth)) / jnp.sqrt(breadth)
    return (profile + jnp.where(distance == 0.0, 1.0, 0.0)).astype(BF16)


def call(kernel, outs, scratch, mebibytes):
    return pl.pallas_call(
        kernel,
        out_shape=outs,
        scratch_shapes=scratch,
        compiler_params=params(mebibytes),
    )


def exchange(rows, wide, axes):
    rows = rows.reshape(TILES, wide, 2, 128).transpose(0, 2, 1, 3).reshape(TILES, 2, wide * 128)
    rows = lax.all_to_all(rows, axes, split_axis=0, concat_axis=0, tiled=True)
    rows = rows.reshape(TILES, 2, wide, 128).transpose(0, 2, 1, 3)
    return rows.reshape(TILES * 2 * wide, 128)


def shape(dims, kind):
    return jax.ShapeDtypeStruct(dims, kind)


def per_device(fractions, cell_index, weights, counts, smoothing, bias_values, observed, precision):
    both = ("slab", "pencil")
    count = lax.axis_size("slab")
    forth = [(i, (i + 1) % count) for i in range(count)]
    aft = [((i + 1) % count, i) for i in range(count)]

    ids = jnp.arange(NY, dtype=jnp.int32)
    breadth = smoothing[:, None, None]
    k_row = correlation(breadth, ids[None, :256, None], ids[None, None, :])
    k_col = correlation(breadth, ids[None, :, None], ids[None, None, :256])
    k_back = correlation(breadth, ids[None, :, None] - 1, ids[None, None, :256])
    rim = jnp.arange(128, dtype=jnp.int32)
    rim_y = (rim // 8 * TY - 1 + rim % 2 * (TY + 1)) % NY
    k_rim = correlation(smoothing[rim % 8 // 2][:, None], rim_y[:, None], ids[None, :])

    table = counts[0].T
    split = [a.reshape(a.shape[0], 128, 128).transpose(1, 0, 2) for a in (fractions, cell_index, weights)]
    mask = pltpu.VMEM((TILES + 8, 128), F32)
    records = call(
        pack_kernel,
        shape((TILES * PAIRS, 128), BF16),
        [pltpu.VMEM((TILES * PAIRS + 16, 128), F32), mask],
        56,
    )(*split, table)
    arrived = exchange(records, PAIRS // 2, both)
    arrived, k_row, k_col, k_back, k_rim = lax.optimization_barrier(
        (arrived, k_row, k_col, k_back, k_rim)
    )
    from_up = lax.ppermute(arrived, "slab", forth)
    from_dn = lax.ppermute(arrived, "slab", aft)
    turned = pltpu.VMEM((RECORD, TILES), F32)
    wide = pltpu.VMEM((TILES * PAIRS + 8, 128), F32)
    places = [pltpu.VMEM((72, 512), F32), pltpu.VMEM((40, 512), F32)]
    acc, xt = call(
        own_kernel,
        (shape((CH, 1040, 128), F32), shape((RECORD, TILES), F32)),
        [wide] + places,
        12,
    )(arrived)
    lines = call(
        forward_kernel,
        shape((N_PENCIL, CHUNK, 128), BF16),
        [pltpu.VMEM((CH, 1040, 128), F32), turned, wide]
        + places
        + [pltpu.VMEM((CH, NZ, 128), BF16), pltpu.VMEM((CH, NZ, 128), F32)],
        24,
    )(from_up, from_dn, acc, k_col)
    lines = lax.all_to_all(lines, "pencil", split_axis=0, concat_axis=0, tiled=True)
    model_field, lines = pl.pallas_call(
        lines_kernel,
        out_shape=(shape((64, NY), BF16), shape((N_PENCIL, CHUNK, 128), BF16)),
        in_specs=[pl.BlockSpec(memory_space=pltpu.SMEM)] + [pl.BlockSpec(memory_space=pltpu.VMEM)] * 5,
        scratch_shapes=[pltpu.VMEM((CH, 256, 256), BF16), pltpu.VMEM((CH, 64, NY), F32)],
        compiler_params=params(20),
    )(bias_values, lines, k_row, k_rim, observed[0], precision[0])
    lines = lax.all_to_all(lines, "pencil", split_axis=0, concat_axis=0, tiled=True)
    fields = []
    for pair in range(2):
        field = call(
            functools.partial(adjoint_kernel, pair),
            shape((NZ + 64, 128), BF16),
            [pltpu.VMEM((2, NZ, 128), BF16), pltpu.VMEM((2, NZ, 128), F32)],
            16,
        )(lines, k_back)
        fields += [field, lax.ppermute(field, "slab", forth), lax.ppermute(field, "slab", aft)]
    sampled = call(
        sample_kernel,
        shape((TILES * BACK, 128), BF16),
        [
            pltpu.VMEM((CH, NZ + 16, 256), BF16),
            pltpu.VMEM((2, 208, 1536), BF16),
            pltpu.VMEM((72, 512), F32),
            pltpu.VMEM((BACK * 128, TILES), F32),
            pltpu.VMEM((TILES * BACK + 8, 128), F32),
        ],
        24,
    )(xt, *fields)
    came_back = lax.all_to_all(
        sampled.reshape(TILES, BACK, 128), both, split_axis=0, concat_axis=0, tiled=True
    ).reshape(TILES * BACK, 128)
    grads = call(
        unpack_kernel,
        shape((128, 7, 128), F32),
        [pltpu.VMEM((TILES * BACK + 8, 128), F32), mask],
        12,
    )(came_back, table)
    return (grads.transpose(1, 0, 2).reshape(7, PART_DEV), model_field[None])


def solution(mesh):
    return jax.shard_map(
        per_device,
        mesh=mesh,
        in_specs=(
            P(None, ("slab", "pencil")),
            P(None, ("slab", "pencil")),
            P(None, ("slab", "pencil")),
            P(("slab", "pencil"), None, None),
            P(),
            P(),
            P("slab", "pencil", None),
            P("slab", "pencil", None),
        ),
        out_specs=(P(None, ("slab", "pencil")), P("slab", "pencil", None)),
        check_vma=False,
    )
```

```python
import functools

import jax
import jax.numpy as jnp
from jax import lax
from jax.experimental import pallas as pl
from jax.experimental.pallas import tpu as pltpu
from jax.sharding import PartitionSpec as P

NY = 1024
NZ = 1024
ZB = 32
PART_DEV = 16384
TILES = 256
CAP = 2
TY = 64
LANES = 64
RECORD = 12 * LANES
GRADS = 7 * LANES
CH = 4
N_PENCIL = 16
CHUNK = 136
F32 = jnp.float32
BF16 = jnp.bfloat16

R_GX, R_GY, R_GZ, R_LOW, R_CY, R_CZ = 4, 5, 6, 3, 10, 11


PAIRS = RECORD // 128
BACK = 4


def params(mebibytes):
    return pltpu.CompilerParams(vmem_limit_bytes=mebibytes * 1024 * 1024)


def lanes_of(shape):
    return lax.broadcasted_iota(jnp.int32, shape, len(shape) - 1)


def live_rows(counts_ref, scr):
    lane = lanes_of((ZB, 128))
    block = lax.broadcasted_iota(jnp.int32, (ZB, 128), 0)
    spread = jnp.where((lane % LANES) // CAP == block, 1.0, 0.0).astype(BF16)
    held = lax.dot_general(
        counts_ref[...].astype(F32).astype(BF16),
        spread,
        (((0,), (0,)), ((), ())),
        preferred_element_type=F32,
    )
    rank = (lanes_of((TILES, 128)) % CAP).astype(F32)
    scr[0:TILES] = jnp.where(rank < held, 1.0, 0.0)
    return scr[pl.ds(0, 128, stride=2), :] > 0.0, scr[pl.ds(1, 128, stride=2), :] > 0.0


def pack_kernel(fr_ref, ci_ref, wt_ref, cn_ref, out_ref, scr, mask):
    low = lanes_of((128, 128)) < LANES
    live = live_rows(cn_ref, mask)

    def put(k, a, b, masked=False):
        even = jnp.where(low, a, pltpu.roll(b, LANES, 1))
        odd = jnp.where(low, pltpu.roll(a, LANES, 1), b)
        if masked:
            even, odd = jnp.where(live[0], even, 0.0), jnp.where(live[1], odd, 0.0)
        scr[pl.ds(k, 128, stride=2 * PAIRS), :] = even
        scr[pl.ds(PAIRS + k, 128, stride=2 * PAIRS), :] = odd

    weights = wt_ref[...].astype(F32)
    put(0, weights[:, 0, :], weights[:, 1, :], True)
    put(1, weights[:, 2, :], weights[:, 3, :], True)
    offsets = [fr_ref[:, d, :] - 0.5 for d in range(3)]
    high = [g.astype(BF16).astype(F32) for g in offsets]
    rest = [g - h for g, h in zip(offsets, high)]
    put(2, high[0], high[1])
    put(3, high[2], rest[0])
    put(4, rest[1], rest[2])
    put(5, ci_ref[:, 1, :].astype(F32), ci_ref[:, 2, :].astype(F32))
    out_ref[...] = scr[0 : TILES * PAIRS].astype(BF16)


def unpack_kernel(in_ref, cn_ref, out_ref, scr, mask):
    low = lanes_of((128, 128)) < LANES
    live = live_rows(cn_ref, mask)
    scr[0 : TILES * BACK] = in_ref[...].astype(F32)
    for j in range(BACK):
        even = jnp.where(live[0], scr[pl.ds(j, 128, stride=2 * BACK), :], 0.0)
        odd = jnp.where(live[1], scr[pl.ds(BACK + j, 128, stride=2 * BACK), :], 0.0)
        out_ref[:, 2 * j, :] = jnp.where(low, even, pltpu.roll(odd, LANES, 1))
        if j < 3:
            out_ref[:, 2 * j + 1, :] = jnp.where(low, pltpu.roll(even, LANES, 1), odd)


def transpose_records(x_ref, wide, xt_ref):
    wide[0 : TILES * PAIRS] = x_ref[...].astype(F32)
    for k in range(PAIRS):
        for h in range(2):
            piece = wide[pl.ds(h * 128 * PAIRS + k, 128, stride=PAIRS), :]
            xt_ref[k * 128 : k * 128 + 128, h * 128 : h * 128 + 128] = piece.T
    first, last = R_GX * LANES, R_GZ * LANES + LANES
    xt_ref[first:last, :] += xt_ref[first + R_LOW * LANES : last + R_LOW * LANES, :]


def slot_row(xt_ref, r, b):
    first = xt_ref[pl.ds(r * LANES + 2 * b, 1), :]
    second = xt_ref[pl.ds(r * LANES + 2 * b + 1, 1), :]
    return jnp.concatenate([first, second], axis=1)


def hat(places, centre):
    return jnp.maximum(1.0 - jnp.abs(places - centre), 0.0)


def rim_places(rows):
    row = lax.broadcasted_iota(jnp.int32, (rows, 128), 0)
    y = jnp.where(row == 64, -1, jnp.where(row == 65, 64, jnp.where(row > 65, 1000, row)))
    return y.astype(F32)


def deposit(xt_ref, acc_ref, yv_ref, zv_ref, side):
    def block(b, carry):
        gx = slot_row(xt_ref, R_GX, b)
        if side == 0:
            wx = 1.0 - jnp.abs(gx)
        elif side < 0:
            wx = jnp.maximum(-gx, 0.0)
        else:
            wx = jnp.maximum(gx, 0.0)
        py = slot_row(xt_ref, R_CY, b) + slot_row(xt_ref, R_GY, b)
        pz = slot_row(xt_ref, R_CZ, b) + slot_row(xt_ref, R_GZ, b) + 1.0
        plane = (wx * hat(yv_ref[...], py)).astype(BF16)
        wz = hat(zv_ref[...], pz)
        column = jnp.concatenate([slot_row(xt_ref, c, b) * wz for c in range(CH)], axis=0).astype(BF16)
        add = lax.dot_general(column, plane, (((1,), (1,)), ((), ())), preferred_element_type=F32)
        at = pl.multiple_of(b * ZB, ZB)
        for c in range(CH):
            acc_ref[c, pl.ds(at, 40), 0:72] += add[c * 40 : c * 40 + 40]
        return carry

    lax.fori_loop(0, NZ // ZB, block, 0, unroll=16)


def fill_places(yv_ref, zv_ref):
    yv = rim_places(72)
    zv = lax.broadcasted_iota(jnp.int32, (40, 128), 0).astype(F32)
    for k in range(4):
        yv_ref[:, k * 128 : k * 128 + 128] = yv
        zv_ref[:, k * 128 : k * 128 + 128] = zv


def own_kernel(x_ref, acc_ref, xt_ref, wide, yv_ref, zv_ref):
    fill_places(yv_ref, zv_ref)
    transpose_records(x_ref, wide, xt_ref)
    acc_ref[...] = jnp.zeros_like(acc_ref)
    deposit(xt_ref, acc_ref, yv_ref, zv_ref, 0)


def along_z(field_ref, col_ref, out_ref, first, count):
    def channel(c, carry):
        quarters = [field_ref[c, i * 256 : i * 256 + 256, :] for i in range(4)]
        pairs = [jnp.concatenate(quarters[i : i + 2], axis=1) for i in (0, 2)]
        right = jnp.concatenate(pairs, axis=0)
        cols = [col_ref[first + c, d * 256 : d * 256 + 256, :] for d in range(4)]
        prods = [
            jnp.dot(
                jnp.concatenate([cols[d], cols[(d - 2) % 4]], axis=1),
                right,
                preferred_element_type=F32,
            )
            for d in range(4)
        ]
        for j in range(4):
            out_ref[c, j * 256 : j * 256 + 256, :] = prods[j][:, 0:128] + prods[(j - 1) % 4][:, 128:256]
        return carry

    lax.fori_loop(0, count, channel, 0, unroll=2)


def rim_rows(parts, rows):
    lane = lanes_of((rows, 128))
    table = jnp.zeros((rows, 128), F32)
    for c, part in enumerate(parts):
        table = jnp.where(lane // 2 == c, pltpu.roll(part, LANES + 2 * c, 1), table)
    return table.T[0:8]


def forward_kernel(up_ref, dn_ref, start_ref, col_ref, out_ref, acc, xt, wide, yv, zv, dens, smooth, cols, sem):
    fetch = pltpu.make_async_copy(col_ref, cols, sem)
    fetch.start()
    fill_places(yv, zv)
    acc[...] = start_ref[...]
    transpose_records(up_ref, wide, xt)
    deposit(xt, acc, yv, zv, 1)
    transpose_records(dn_ref, wide, xt)
    deposit(xt, acc, yv, zv, -1)
    acc[:, NZ : NZ + 1, :] += acc[:, 0:1, :]
    acc[:, 1:2, :] += acc[:, NZ + 1 : NZ + 2, :]
    dens[...] = acc[:, 1 : NZ + 1, :].astype(BF16)
    fetch.wait()
    along_z(dens, cols, smooth, 0, CH)
    low = lanes_of((64, 128)) < LANES

    def send(p, carry):
        at = pl.multiple_of(p * 64, 64)
        parts = [smooth[c, pl.ds(at, 64), :] for c in range(CH)]
        for pair in range(2):
            both = jnp.where(low, parts[2 * pair], pltpu.roll(parts[2 * pair + 1], LANES, 1))
            out_ref[p, pair * 64 : pair * 64 + 64, :] = both.astype(BF16)
        rims = rim_rows(parts, 64)
        out_ref[p, 128:136, :] = jnp.concatenate([rims, jnp.zeros((8, 64), F32)], axis=1).astype(BF16)
        return carry

    lax.fori_loop(0, N_PENCIL, send, 0, unroll=16)


def wrapped_sum(prod):
    blocks = []
    for j in range(4):
        total = prod[0:64, j * 256 : j * 256 + 256]
        for i in range(1, 4):
            d = (j - i) % 4
            total = total + prod[i * 64 : i * 64 + 64, d * 256 : d * 256 + 256]
        blocks.append(total)
    return jnp.concatenate(blocks, axis=1)


def lines_kernel(bias_ref, in_ref, row_ref, rim_ref, obs_ref, prec_ref, model_ref, out_ref, left, back):
    low = lanes_of((64, 128)) < LANES
    for pair in range(2):
        for pp in range(8):
            a = in_ref[2 * pp, pair * 64 : pair * 64 + 64, :].astype(F32)
            b = in_ref[2 * pp + 1, pair * 64 : pair * 64 + 64, :].astype(F32)
            i, at = pp // 2, (pp % 2) * 128
            left[2 * pair, i * 64 : i * 64 + 64, at : at + 128] = jnp.where(
                low, a, pltpu.roll(b, LANES, 1)
            ).astype(BF16)
            left[2 * pair + 1, i * 64 : i * 64 + 64, at : at + 128] = jnp.where(
                low, pltpu.roll(a, LANES, 1), b
            ).astype(BF16)
    which = lax.broadcasted_iota(jnp.int32, (128, 64), 0) % 8 // 2
    bias = jnp.zeros((128, 64), F32)
    for c in range(CH):
        bias = jnp.where(which == c, bias_ref[c], bias)
    rims = jnp.concatenate([in_ref[p, 128:136, 0:64].astype(F32) for p in range(N_PENCIL)], axis=0)
    rims = (rims * bias).T.astype(BF16)
    model = jnp.dot(rims, rim_ref[...], preferred_element_type=F32)
    for c in range(CH):
        prod = jnp.dot(left[c], row_ref[c], preferred_element_type=F32)
        model = model + bias_ref[c] * wrapped_sum(prod)
    model_ref[...] = model.astype(BF16)
    pull = (prec_ref[...] * (model - obs_ref[...])).astype(BF16)
    stacked = jnp.concatenate([pull[:, i * 256 : i * 256 + 256] for i in range(4)], axis=0)
    for c in range(CH):
        prod = jnp.dot(stacked, row_ref[c], preferred_element_type=F32)
        back[c] = bias_ref[c] * wrapped_sum(prod)
    for pair in range(2):
        for pp in range(8):
            a = back[2 * pair, :, pp * 128 : pp * 128 + 128]
            b = back[2 * pair + 1, :, pp * 128 : pp * 128 + 128]
            out_ref[2 * pp, pair * 64 : pair * 64 + 64, :] = jnp.where(
                low, a, pltpu.roll(b, LANES, 1)
            ).astype(BF16)
            out_ref[2 * pp + 1, pair * 64 : pair * 64 + 64, :] = jnp.where(
                low, pltpu.roll(a, LANES, 1), b
            ).astype(BF16)
    rims = lax.dot_general(rim_ref[...], pull, (((1,), (1,)), ((), ())), preferred_element_type=F32)
    rims = jnp.concatenate([rims * bias, jnp.zeros((128, 64), F32)], axis=1).astype(BF16)
    for p in range(N_PENCIL):
        out_ref[p, 128:136, :] = rims[p * 8 : p * 8 + 8]


def adjoint_kernel(pair, in_ref, col_ref, out_ref, field, smooth):
    lane = lanes_of((64, 128))
    low = lane < LANES

    def take(p, carry):
        at = pl.multiple_of(p * 64, 64)
        rims = in_ref[p, 128:136, :].astype(F32)
        table = jnp.concatenate([rims, jnp.zeros((120, 128), F32)], axis=0).T[0:64]
        both = in_ref[p, pair * 64 : pair * 64 + 64, :].astype(F32)
        for k in range(2):
            main = both if k == 0 else pltpu.roll(both, LANES, 1)
            rim = jnp.where(lane < 66, pltpu.roll(table, LANES - 2 * (2 * pair + k), 1), 0.0)
            field[k, pl.ds(at, 64), :] = jnp.where(low, main, rim).astype(BF16)
        return carry

    lax.fori_loop(0, N_PENCIL, take, 0, unroll=4)
    along_z(field, col_ref, smooth, 2 * pair, 2)
    wide = lanes_of((128, 128)) < LANES
    for q in range(8):
        parts = [smooth[k, q * 128 : q * 128 + 128, :] for k in range(2)]
        both = jnp.where(wide, parts[0], pltpu.roll(parts[1], LANES, 1))
        out_ref[q * 128 : q * 128 + 128, :] = both.astype(BF16)
        out_ref[NZ + q * 8 : NZ + q * 8 + 8, :] = rim_rows(parts, 128).astype(BF16)


def write_planes(xt_ref, b, places, planes):
    gx, gy, cy = (slot_row(xt_ref, r, b) for r in (R_GX, R_GY, R_CY))
    fall_x, fall_y = gx < 0.0, gy < 0.0
    wx = [jnp.maximum(-gx, 0.0), jnp.maximum(gx, 0.0), 1.0 - jnp.abs(gx)]
    sx = [jnp.where(fall_x, -1.0, 0.0), jnp.where(fall_x, 0.0, 1.0), jnp.where(fall_x, 1.0, -1.0)]
    wy = hat(places, cy + gy)
    step_y = places - jnp.where(fall_y, cy - 1.0, cy)
    sy = jnp.where(step_y == 0.0, -1.0, jnp.where(step_y == 1.0, 1.0, 0.0))
    wx16, sx16 = ([a.astype(BF16) for a in ax] for ax in (wx, sx))
    wy16, sy16 = wy[0:64].astype(BF16), sy[0:64].astype(BF16)
    for s in range(3):
        rows = slice(s * 64, s * 64 + 64)
        planes[rows, 0:512] = (wx[s] * wy[0:64]).astype(BF16)
        planes[rows, 512:1024] = sx16[s] * wy16
        planes[rows, 1024:1536] = wx16[s] * sy16
    part = lax.broadcasted_iota(jnp.int32, (8, 512), 0) // 2
    for k, (ax, ay) in enumerate(((wx, wy), (sx, wy), (wx, sy))):
        rim = jnp.where(
            part == 0, ax[2], jnp.where(part == 1, ax[0], jnp.where(part == 2, ax[1], 0.0))
        )
        rim = jnp.concatenate([rim * ay[64:72], jnp.zeros((8, 512), F32)], axis=0)
        planes[192:208, k * 512 : k * 512 + 512] = rim.astype(BF16)


def weights_kernel(xt_ref, planes, yv):
    row = lax.broadcasted_iota(jnp.int32, (72, 512), 0)
    yv[...] = jnp.where(row < 64, row, jnp.where(row % 2 == 0, -1, 64)).astype(F32)

    def block(b, carry):
        write_planes(xt_ref, b, yv[...], planes.at[b])
        return carry

    lax.fori_loop(0, NZ // ZB, block, 0, unroll=2)


def fill_field(refs, field):
    lane = lanes_of((128, 128))
    low = lane < LANES

    def fill(q, carry):
        at = pl.multiple_of(q * 128, 128)
        rim_at = pl.multiple_of(NZ + q * 8, 8)
        for pair in range(2):
            tables = []
            for ref in refs[pair]:
                rims = ref[pl.ds(rim_at, 8), :].astype(F32)
                tables.append(jnp.concatenate([rims, jnp.zeros((120, 128), F32)], axis=0).T)
            own, up, dn = (ref[pl.ds(at, 128), :].astype(F32) for ref in refs[pair])
            for k in range(2):
                c = 2 * pair + k
                if k == 0:
                    first = jnp.where(low, up, pltpu.roll(dn, LANES, 1))
                    main = own
                else:
                    first = jnp.where(low, pltpu.roll(up, LANES, 1), dn)
                    main = pltpu.roll(own, LANES, 1)
                rim = jnp.zeros((128, 128), F32)
                for s in range(3):
                    here = pltpu.roll(tables[s], LANES + 2 * s - 2 * k, 1)
                    rim = jnp.where((lane - LANES) // 2 == s, here, rim)
                field[c, pl.ds(at, 128), 0:128] = first.astype(BF16)
                field[c, pl.ds(at, 128), 128:256] = jnp.where(low, main, rim).astype(BF16)
        return carry

    lax.fori_loop(0, 8, fill, 0, unroll=8)
    field[:, NZ : NZ + 16, :] = field[:, 0:16, :]


def sample_kernel(planes, xt_ref, *rest):
    refs, (out_ref, field, ot, tall) = (rest[0:3], rest[3:6]), rest[6:]
    fill_field(refs, field)
    zv = lax.broadcasted_iota(jnp.int32, (40, 512), 0).astype(F32)
    ot[GRADS:, :] = jnp.zeros((LANES, TILES), F32)

    def block(b, carry):
        gz, cz = slot_row(xt_ref, R_GZ, b), slot_row(xt_ref, R_CZ, b)
        at = pl.multiple_of(b * ZB, ZB)
        here = jnp.concatenate([field[c, pl.ds(at, 48), :] for c in range(CH)], axis=0)
        wz = hat(zv, cz + gz + 1.0)
        step_z = zv - jnp.where(gz < 0.0, cz, cz + 1.0)
        sz = jnp.where(step_z == 0.0, -1.0, jnp.where(step_z == 1.0, 1.0, 0.0))
        masses = [slot_row(xt_ref, c, b) for c in range(CH)]
        grads = []
        for k in range(3):
            sampled = jnp.dot(
                here[:, 0:208], planes[b, :, k * 512 : k * 512 + 512], preferred_element_type=F32
            )
            total = jnp.zeros((40, 512), F32)
            for c in range(CH):
                v = sampled[c * 48 : c * 48 + 40]
                if k == 0:
                    grads.append(jnp.sum(v * wz, axis=0, keepdims=True))
                total = total + masses[c] * v
            if k == 0:
                slope_z = jnp.sum(total * sz, axis=0, keepdims=True)
            else:
                grads.append(jnp.sum(total * wz, axis=0, keepdims=True))
        grads.append(slope_z)
        for r in range(7):
            ot[pl.ds(r * LANES + 2 * b, 1), :] = grads[r][:, 0:256]
            ot[pl.ds(r * LANES + 2 * b + 1, 1), :] = grads[r][:, 256:512]
        return carry

    lax.fori_loop(0, NZ // ZB, block, 0, unroll=2)
    for j in range(BACK):
        for h in range(2):
            piece = ot[j * 128 : j * 128 + 128, h * 128 : h * 128 + 128]
            tall[pl.ds(h * 128 * BACK + j, 128, stride=BACK), :] = piece.T
    out_ref[...] = tall[0 : TILES * BACK].astype(BF16)


def correlation(smoothing, rows, columns):
    distance = jnp.abs(rows - columns)
    distance = jnp.minimum(distance, NY - distance).astype(F32)
    breadth = smoothing
    profile = jnp.exp(-distance * distance / (2.0 * breadth * breadth)) / jnp.sqrt(breadth)
    return (profile + jnp.where(distance == 0.0, 1.0, 0.0)).astype(BF16)


def call(kernel, outs, scratch, mebibytes):
    return pl.pallas_call(
        kernel,
        out_shape=outs,
        scratch_shapes=scratch,
        compiler_params=params(mebibytes),
    )


def exchange(rows, wide, axes):
    rows = rows.reshape(TILES, wide, 2, 128).transpose(0, 2, 1, 3).reshape(TILES, 2, wide * 128)
    rows = lax.all_to_all(rows, axes, split_axis=0, concat_axis=0, tiled=True)
    rows = rows.reshape(TILES, 2, wide, 128).transpose(0, 2, 1, 3)
    return rows.reshape(TILES * 2 * wide, 128)


def shape(dims, kind):
    return jax.ShapeDtypeStruct(dims, kind)


def per_device(fractions, cell_index, weights, counts, smoothing, bias_values, observed, precision):
    both = ("slab", "pencil")
    count = lax.axis_size("slab")
    forth = [(i, (i + 1) % count) for i in range(count)]
    aft = [((i + 1) % count, i) for i in range(count)]

    ids = jnp.arange(NY, dtype=jnp.int32)
    breadth = smoothing[:, None, None]
    k_row = correlation(breadth, ids[None, :256, None], ids[None, None, :])
    k_col = correlation(breadth, ids[None, :, None], ids[None, None, :256])
    k_back = correlation(breadth, ids[None, :, None] - 1, ids[None, None, :256])
    rim = jnp.arange(128, dtype=jnp.int32)
    rim_y = (rim // 8 * TY - 1 + rim % 2 * (TY + 1)) % NY
    k_rim = correlation(smoothing[rim % 8 // 2][:, None], rim_y[:, None], ids[None, :])

    table = counts[0].T
    split = [a.reshape(a.shape[0], 128, 128).transpose(1, 0, 2) for a in (fractions, cell_index, weights)]
    mask = pltpu.VMEM((TILES + 8, 128), F32)
    records = call(
        pack_kernel,
        shape((TILES * PAIRS, 128), BF16),
        [pltpu.VMEM((TILES * PAIRS + 16, 128), F32), mask],
        56,
    )(*split, table)
    arrived = exchange(records, PAIRS // 2, both)
    arrived, k_row, k_col, k_back, k_rim = lax.optimization_barrier(
        (arrived, k_row, k_col, k_back, k_rim)
    )
    from_up = lax.ppermute(arrived, "slab", forth)
    from_dn = lax.ppermute(arrived, "slab", aft)
    turned = pltpu.VMEM((RECORD, TILES), F32)
    wide = pltpu.VMEM((TILES * PAIRS + 8, 128), F32)
    places = [pltpu.VMEM((72, 512), F32), pltpu.VMEM((40, 512), F32)]
    acc, xt = call(
        own_kernel,
        (shape((CH, 1040, 128), F32), shape((RECORD, TILES), F32)),
        [wide] + places,
        12,
    )(arrived)
    whole = pl.BlockSpec(memory_space=pltpu.VMEM)
    lines = pl.pallas_call(
        forward_kernel,
        out_shape=shape((N_PENCIL, CHUNK, 128), BF16),
        in_specs=[whole] * 3 + [pl.BlockSpec(memory_space=pltpu.HBM)],
        scratch_shapes=[pltpu.VMEM((CH, 1040, 128), F32), turned, wide]
        + places
        + [
            pltpu.VMEM((CH, NZ, 128), BF16),
            pltpu.VMEM((CH, NZ, 128), F32),
            pltpu.VMEM((CH, NZ, 256), BF16),
            pltpu.SemaphoreType.DMA,
        ],
        compiler_params=params(24),
    )(from_up, from_dn, acc, pltpu.with_memory_space_constraint(k_col, pltpu.HBM))
    lines = lax.all_to_all(lines, "pencil", split_axis=0, concat_axis=0, tiled=True)
    model_field, lines = pl.pallas_call(
        lines_kernel,
        out_shape=(shape((64, NY), BF16), shape((N_PENCIL, CHUNK, 128), BF16)),
        in_specs=[pl.BlockSpec(memory_space=pltpu.SMEM)] + [pl.BlockSpec(memory_space=pltpu.VMEM)] * 5,
        scratch_shapes=[pltpu.VMEM((CH, 256, 256), BF16), pltpu.VMEM((CH, 64, NY), F32)],
        compiler_params=params(20),
    )(bias_values, lines, k_row, k_rim, observed[0], precision[0])
    lines = lax.all_to_all(lines, "pencil", split_axis=0, concat_axis=0, tiled=True)
    fields = []
    for pair in range(2):
        field = call(
            functools.partial(adjoint_kernel, pair),
            shape((NZ + 64, 128), BF16),
            [pltpu.VMEM((2, NZ, 128), BF16), pltpu.VMEM((2, NZ, 128), F32)],
            16,
        )(lines, k_back)
        if pair == 1:
            field, late = lax.optimization_barrier((field, xt))
        fields += [field, lax.ppermute(field, "slab", forth), lax.ppermute(field, "slab", aft)]
    planes = pl.pallas_call(
        weights_kernel,
        out_shape=shape((NZ // ZB, 208, 1536), BF16),
        scratch_shapes=[pltpu.VMEM((72, 512), F32)],
        compiler_params=params(22),
        cost_estimate=pl.CostEstimate(flops=60_000_000, bytes_accessed=21_000_000, transcendentals=0),
    )(late)
    sampled = call(
        sample_kernel,
        shape((TILES * BACK, 128), BF16),
        [
            pltpu.VMEM((CH, NZ + 16, 256), BF16),
            pltpu.VMEM((BACK * 128, TILES), F32),
            pltpu.VMEM((TILES * BACK + 8, 128), F32),
        ],
        30,
    )(planes, xt, *fields)
    came_back = lax.all_to_all(
        sampled.reshape(TILES, BACK, 128), both, split_axis=0, concat_axis=0, tiled=True
    ).reshape(TILES * BACK, 128)
    grads = call(
        unpack_kernel,
        shape((128, 7, 128), F32),
        [pltpu.VMEM((TILES * BACK + 8, 128), F32), mask],
        12,
    )(came_back, table)
    return (grads.transpose(1, 0, 2).reshape(7, PART_DEV), model_field[None])


def solution(mesh):
    return jax.shard_map(
        per_device,
        mesh=mesh,
        in_specs=(
            P(None, ("slab", "pencil")),
            P(None, ("slab", "pencil")),
            P(None, ("slab", "pencil")),
            P(("slab", "pencil"), None, None),
            P(),
            P(),
            P("slab", "pencil", None),
            P("slab", "pencil", None),
        ),
        out_specs=(P(None, ("slab", "pencil")), P("slab", "pencil", None)),
        check_vma=False,
    )
```

```python
import functools

import jax
import jax.numpy as jnp
from jax import lax
from jax.experimental import pallas as pl
from jax.experimental.pallas import tpu as pltpu
from jax.sharding import PartitionSpec as P

NY = 1024
NZ = 1024
ZB = 32
PART_DEV = 16384
TILES = 256
CAP = 2
TY = 64
LANES = 64
RECORD = 12 * LANES
GRADS = 7 * LANES
CH = 4
N_PENCIL = 16
CHUNK = 136
F32 = jnp.float32
BF16 = jnp.bfloat16

R_GX, R_GY, R_GZ, R_LOW, R_CY, R_CZ = 4, 5, 6, 3, 10, 11


PAIRS = RECORD // 128
BACK = 4


def params(mebibytes):
    return pltpu.CompilerParams(vmem_limit_bytes=mebibytes * 1024 * 1024)


def lanes_of(shape):
    return lax.broadcasted_iota(jnp.int32, shape, len(shape) - 1)


def live_rows(counts_ref, scr):
    lane = lanes_of((ZB, 128))
    block = lax.broadcasted_iota(jnp.int32, (ZB, 128), 0)
    spread = jnp.where((lane % LANES) // CAP == block, 1.0, 0.0).astype(BF16)
    held = lax.dot_general(
        counts_ref[...].astype(F32).astype(BF16),
        spread,
        (((0,), (0,)), ((), ())),
        preferred_element_type=F32,
    )
    rank = (lanes_of((TILES, 128)) % CAP).astype(F32)
    scr[0:TILES] = jnp.where(rank < held, 1.0, 0.0)
    return scr[pl.ds(0, 128, stride=2), :] > 0.0, scr[pl.ds(1, 128, stride=2), :] > 0.0


def pack_kernel(fr_ref, ci_ref, wt_ref, cn_ref, out_ref, scr, mask):
    low = lanes_of((128, 128)) < LANES
    live = live_rows(cn_ref, mask)

    def put(k, a, b, masked=False):
        even = jnp.where(low, a, pltpu.roll(b, LANES, 1))
        odd = jnp.where(low, pltpu.roll(a, LANES, 1), b)
        if masked:
            even, odd = jnp.where(live[0], even, 0.0), jnp.where(live[1], odd, 0.0)
        scr[pl.ds(k, 128, stride=2 * PAIRS), :] = even
        scr[pl.ds(PAIRS + k, 128, stride=2 * PAIRS), :] = odd

    weights = wt_ref[...].astype(F32)
    put(0, weights[:, 0, :], weights[:, 1, :], True)
    put(1, weights[:, 2, :], weights[:, 3, :], True)
    offsets = [fr_ref[:, d, :] - 0.5 for d in range(3)]
    high = [g.astype(BF16).astype(F32) for g in offsets]
    rest = [g - h for g, h in zip(offsets, high)]
    put(2, high[0], high[1])
    put(3, high[2], rest[0])
    put(4, rest[1], rest[2])
    put(5, ci_ref[:, 1, :].astype(F32), ci_ref[:, 2, :].astype(F32))
    out_ref[...] = scr[0 : TILES * PAIRS].astype(BF16)


def unpack_kernel(in_ref, cn_ref, out_ref, scr, mask):
    low = lanes_of((128, 128)) < LANES
    live = live_rows(cn_ref, mask)
    scr[0 : TILES * BACK] = in_ref[...].astype(F32)
    for j in range(BACK):
        even = jnp.where(live[0], scr[pl.ds(j, 128, stride=2 * BACK), :], 0.0)
        odd = jnp.where(live[1], scr[pl.ds(BACK + j, 128, stride=2 * BACK), :], 0.0)
        out_ref[:, 2 * j, :] = jnp.where(low, even, pltpu.roll(odd, LANES, 1))
        if j < 3:
            out_ref[:, 2 * j + 1, :] = jnp.where(low, pltpu.roll(even, LANES, 1), odd)


def transpose_records(x_ref, wide, xt_ref):
    wide[0 : TILES * PAIRS] = x_ref[...].astype(F32)
    for k in range(PAIRS):
        for h in range(2):
            piece = wide[pl.ds(h * 128 * PAIRS + k, 128, stride=PAIRS), :]
            xt_ref[k * 128 : k * 128 + 128, h * 128 : h * 128 + 128] = piece.T
    first, last = R_GX * LANES, R_GZ * LANES + LANES
    xt_ref[first:last, :] += xt_ref[first + R_LOW * LANES : last + R_LOW * LANES, :]


def slot_row(xt_ref, r, b):
    first = xt_ref[pl.ds(r * LANES + 2 * b, 1), :]
    second = xt_ref[pl.ds(r * LANES + 2 * b + 1, 1), :]
    return jnp.concatenate([first, second], axis=1)


def hat(places, centre):
    return jnp.maximum(1.0 - jnp.abs(places - centre), 0.0)


def rim_places(rows):
    row = lax.broadcasted_iota(jnp.int32, (rows, 128), 0)
    y = jnp.where(row == 64, -1, jnp.where(row == 65, 64, jnp.where(row > 65, 1000, row)))
    return y.astype(F32)


def deposit(xt_ref, acc_ref, yv_ref, zv_ref, side):
    def block(b, carry):
        gx = slot_row(xt_ref, R_GX, b)
        if side == 0:
            wx = 1.0 - jnp.abs(gx)
        elif side < 0:
            wx = jnp.maximum(-gx, 0.0)
        else:
            wx = jnp.maximum(gx, 0.0)
        py = slot_row(xt_ref, R_CY, b) + slot_row(xt_ref, R_GY, b)
        pz = slot_row(xt_ref, R_CZ, b) + slot_row(xt_ref, R_GZ, b) + 1.0
        plane = (wx * hat(yv_ref[...], py)).astype(BF16)
        wz = hat(zv_ref[...], pz)
        column = jnp.concatenate([slot_row(xt_ref, c, b) * wz for c in range(CH)], axis=0).astype(BF16)
        add = lax.dot_general(column, plane, (((1,), (1,)), ((), ())), preferred_element_type=F32)
        at = pl.multiple_of(b * ZB, ZB)
        for c in range(CH):
            acc_ref[c, pl.ds(at, 40), 0:72] += add[c * 40 : c * 40 + 40]
        return carry

    lax.fori_loop(0, NZ // ZB, block, 0, unroll=32)


def fill_places(yv_ref, zv_ref):
    yv = rim_places(72)
    zv = lax.broadcasted_iota(jnp.int32, (40, 128), 0).astype(F32)
    for k in range(4):
        yv_ref[:, k * 128 : k * 128 + 128] = yv
        zv_ref[:, k * 128 : k * 128 + 128] = zv


def own_kernel(x_ref, acc_ref, xt_ref, wide, yv_ref, zv_ref):
    fill_places(yv_ref, zv_ref)
    transpose_records(x_ref, wide, xt_ref)
    acc_ref[...] = jnp.zeros_like(acc_ref)
    deposit(xt_ref, acc_ref, yv_ref, zv_ref, 0)


def along_z(field_ref, col_ref, out_ref, first, count):
    def channel(c, carry):
        quarters = [field_ref[c, i * 256 : i * 256 + 256, :] for i in range(4)]
        pairs = [jnp.concatenate(quarters[i : i + 2], axis=1) for i in (0, 2)]
        right = jnp.concatenate(pairs, axis=0)
        cols = [col_ref[first + c, d * 256 : d * 256 + 256, :] for d in range(4)]
        prods = [
            jnp.dot(
                jnp.concatenate([cols[d], cols[(d - 2) % 4]], axis=1),
                right,
                preferred_element_type=F32,
            )
            for d in range(4)
        ]
        for j in range(4):
            out_ref[c, j * 256 : j * 256 + 256, :] = prods[j][:, 0:128] + prods[(j - 1) % 4][:, 128:256]
        return carry

    lax.fori_loop(0, count, channel, 0, unroll=2)


def rim_rows(parts, rows):
    lane = lanes_of((rows, 128))
    table = jnp.zeros((rows, 128), F32)
    for c, part in enumerate(parts):
        table = jnp.where(lane // 2 == c, pltpu.roll(part, LANES + 2 * c, 1), table)
    return table.T[0:8]


def forward_kernel(up_ref, dn_ref, start_ref, col_ref, out_ref, acc, xt, wide, yv, zv, dens, smooth, cols, sem):
    fetch = pltpu.make_async_copy(col_ref, cols, sem)
    fetch.start()
    fill_places(yv, zv)
    acc[...] = start_ref[...]
    transpose_records(up_ref, wide, xt)
    deposit(xt, acc, yv, zv, 1)
    transpose_records(dn_ref, wide, xt)
    deposit(xt, acc, yv, zv, -1)
    acc[:, NZ : NZ + 1, :] += acc[:, 0:1, :]
    acc[:, 1:2, :] += acc[:, NZ + 1 : NZ + 2, :]
    dens[...] = acc[:, 1 : NZ + 1, :].astype(BF16)
    fetch.wait()
    along_z(dens, cols, smooth, 0, CH)
    low = lanes_of((64, 128)) < LANES

    def send(p, carry):
        at = pl.multiple_of(p * 64, 64)
        parts = [smooth[c, pl.ds(at, 64), :] for c in range(CH)]
        for pair in range(2):
            both = jnp.where(low, parts[2 * pair], pltpu.roll(parts[2 * pair + 1], LANES, 1))
            out_ref[p, pair * 64 : pair * 64 + 64, :] = both.astype(BF16)
        rims = rim_rows(parts, 64)
        out_ref[p, 128:136, :] = jnp.concatenate([rims, jnp.zeros((8, 64), F32)], axis=1).astype(BF16)
        return carry

    lax.fori_loop(0, N_PENCIL, send, 0, unroll=16)


def wrapped_sum(prod):
    blocks = []
    for j in range(4):
        total = prod[0:64, j * 256 : j * 256 + 256]
        for i in range(1, 4):
            d = (j - i) % 4
            total = total + prod[i * 64 : i * 64 + 64, d * 256 : d * 256 + 256]
        blocks.append(total)
    return jnp.concatenate(blocks, axis=1)


def lines_kernel(bias_ref, in_ref, row_ref, rim_ref, obs_ref, prec_ref, model_ref, out_ref, left, back):
    low = lanes_of((64, 128)) < LANES
    for pair in range(2):
        for pp in range(8):
            a = in_ref[2 * pp, pair * 64 : pair * 64 + 64, :].astype(F32)
            b = in_ref[2 * pp + 1, pair * 64 : pair * 64 + 64, :].astype(F32)
            i, at = pp // 2, (pp % 2) * 128
            left[2 * pair, i * 64 : i * 64 + 64, at : at + 128] = jnp.where(
                low, a, pltpu.roll(b, LANES, 1)
            ).astype(BF16)
            left[2 * pair + 1, i * 64 : i * 64 + 64, at : at + 128] = jnp.where(
                low, pltpu.roll(a, LANES, 1), b
            ).astype(BF16)
    which = lax.broadcasted_iota(jnp.int32, (128, 64), 0) % 8 // 2
    bias = jnp.zeros((128, 64), F32)
    for c in range(CH):
        bias = jnp.where(which == c, bias_ref[c], bias)
    rims = jnp.concatenate([in_ref[p, 128:136, 0:64].astype(F32) for p in range(N_PENCIL)], axis=0)
    rims = (rims * bias).T.astype(BF16)
    model = jnp.dot(rims, rim_ref[...], preferred_element_type=F32)
    for c in range(CH):
        prod = jnp.dot(left[c], row_ref[c], preferred_element_type=F32)
        model = model + bias_ref[c] * wrapped_sum(prod)
    model_ref[...] = model.astype(BF16)
    pull = (prec_ref[...] * (model - obs_ref[...])).astype(BF16)
    stacked = jnp.concatenate([pull[:, i * 256 : i * 256 + 256] for i in range(4)], axis=0)
    for c in range(CH):
        prod = jnp.dot(stacked, row_ref[c], preferred_element_type=F32)
        back[c] = bias_ref[c] * wrapped_sum(prod)
    for pair in range(2):
        for pp in range(8):
            a = back[2 * pair, :, pp * 128 : pp * 128 + 128]
            b = back[2 * pair + 1, :, pp * 128 : pp * 128 + 128]
            out_ref[2 * pp, pair * 64 : pair * 64 + 64, :] = jnp.where(
                low, a, pltpu.roll(b, LANES, 1)
            ).astype(BF16)
            out_ref[2 * pp + 1, pair * 64 : pair * 64 + 64, :] = jnp.where(
                low, pltpu.roll(a, LANES, 1), b
            ).astype(BF16)
    rims = lax.dot_general(rim_ref[...], pull, (((1,), (1,)), ((), ())), preferred_element_type=F32)
    rims = jnp.concatenate([rims * bias, jnp.zeros((128, 64), F32)], axis=1).astype(BF16)
    for p in range(N_PENCIL):
        out_ref[p, 128:136, :] = rims[p * 8 : p * 8 + 8]


def adjoint_kernel(pair, in_ref, col_ref, out_ref, field, smooth):
    lane = lanes_of((64, 128))
    low = lane < LANES

    def take(p, carry):
        at = pl.multiple_of(p * 64, 64)
        rims = in_ref[p, 128:136, :].astype(F32)
        table = jnp.concatenate([rims, jnp.zeros((120, 128), F32)], axis=0).T[0:64]
        both = in_ref[p, pair * 64 : pair * 64 + 64, :].astype(F32)
        for k in range(2):
            main = both if k == 0 else pltpu.roll(both, LANES, 1)
            rim = jnp.where(lane < 66, pltpu.roll(table, LANES - 2 * (2 * pair + k), 1), 0.0)
            field[k, pl.ds(at, 64), :] = jnp.where(low, main, rim).astype(BF16)
        return carry

    lax.fori_loop(0, N_PENCIL, take, 0, unroll=16)
    along_z(field, col_ref, smooth, 2 * pair, 2)
    wide = lanes_of((128, 128)) < LANES
    for q in range(8):
        parts = [smooth[k, q * 128 : q * 128 + 128, :] for k in range(2)]
        both = jnp.where(wide, parts[0], pltpu.roll(parts[1], LANES, 1))
        out_ref[q * 128 : q * 128 + 128, :] = both.astype(BF16)
        out_ref[NZ + q * 8 : NZ + q * 8 + 8, :] = rim_rows(parts, 128).astype(BF16)


def write_planes(xt_ref, b, places, planes):
    gx, gy, cy = (slot_row(xt_ref, r, b) for r in (R_GX, R_GY, R_CY))
    fall_x, fall_y = gx < 0.0, gy < 0.0
    wx = [jnp.maximum(-gx, 0.0), jnp.maximum(gx, 0.0), 1.0 - jnp.abs(gx)]
    sx = [jnp.where(fall_x, -1.0, 0.0), jnp.where(fall_x, 0.0, 1.0), jnp.where(fall_x, 1.0, -1.0)]
    wy = hat(places, cy + gy)
    step_y = places - jnp.where(fall_y, cy - 1.0, cy)
    sy = jnp.where(step_y == 0.0, -1.0, jnp.where(step_y == 1.0, 1.0, 0.0))
    wx16, sx16 = ([a.astype(BF16) for a in ax] for ax in (wx, sx))
    wy16, sy16 = wy[0:64].astype(BF16), sy[0:64].astype(BF16)
    for s in range(3):
        rows = slice(s * 64, s * 64 + 64)
        planes[rows, 0:512] = (wx[s] * wy[0:64]).astype(BF16)
        planes[rows, 512:1024] = sx16[s] * wy16
        planes[rows, 1024:1536] = wx16[s] * sy16
    part = lax.broadcasted_iota(jnp.int32, (8, 512), 0) // 2
    for k, (ax, ay) in enumerate(((wx, wy), (sx, wy), (wx, sy))):
        rim = jnp.where(
            part == 0, ax[2], jnp.where(part == 1, ax[0], jnp.where(part == 2, ax[1], 0.0))
        )
        rim = jnp.concatenate([rim * ay[64:72], jnp.zeros((8, 512), F32)], axis=0)
        planes[192:208, k * 512 : k * 512 + 512] = rim.astype(BF16)


def weights_kernel(xt_ref, planes, yv):
    row = lax.broadcasted_iota(jnp.int32, (72, 512), 0)
    yv[...] = jnp.where(row < 64, row, jnp.where(row % 2 == 0, -1, 64)).astype(F32)

    def block(b, carry):
        write_planes(xt_ref, b, yv[...], planes.at[b])
        return carry

    lax.fori_loop(0, NZ // ZB, block, 0, unroll=2)


def fill_field(refs, field):
    lane = lanes_of((128, 128))
    low = lane < LANES

    def fill(q, carry):
        at = pl.multiple_of(q * 128, 128)
        rim_at = pl.multiple_of(NZ + q * 8, 8)
        for pair in range(2):
            tables = []
            for ref in refs[pair]:
                rims = ref[pl.ds(rim_at, 8), :].astype(F32)
                tables.append(jnp.concatenate([rims, jnp.zeros((120, 128), F32)], axis=0).T)
            own, up, dn = (ref[pl.ds(at, 128), :].astype(F32) for ref in refs[pair])
            for k in range(2):
                c = 2 * pair + k
                if k == 0:
                    first = jnp.where(low, up, pltpu.roll(dn, LANES, 1))
                    main = own
                else:
                    first = jnp.where(low, pltpu.roll(up, LANES, 1), dn)
                    main = pltpu.roll(own, LANES, 1)
                rim = jnp.zeros((128, 128), F32)
                for s in range(3):
                    here = pltpu.roll(tables[s], LANES + 2 * s - 2 * k, 1)
                    rim = jnp.where((lane - LANES) // 2 == s, here, rim)
                field[c, pl.ds(at, 128), 0:128] = first.astype(BF16)
                field[c, pl.ds(at, 128), 128:256] = jnp.where(low, main, rim).astype(BF16)
        return carry

    lax.fori_loop(0, 8, fill, 0, unroll=8)
    field[:, NZ : NZ + 16, :] = field[:, 0:16, :]


def sample_kernel(planes, xt_ref, *rest):
    refs, (out_ref, field, ot, tall) = (rest[0:3], rest[3:6]), rest[6:]
    fill_field(refs, field)
    zv = lax.broadcasted_iota(jnp.int32, (40, 512), 0).astype(F32)
    ot[GRADS:, :] = jnp.zeros((LANES, TILES), F32)

    def block(b, carry):
        gz, cz = slot_row(xt_ref, R_GZ, b), slot_row(xt_ref, R_CZ, b)
        at = pl.multiple_of(b * ZB, ZB)
        here = jnp.concatenate([field[c, pl.ds(at, 48), :] for c in range(CH)], axis=0)
        wz = hat(zv, cz + gz + 1.0)
        step_z = zv - jnp.where(gz < 0.0, cz, cz + 1.0)
        sz = jnp.where(step_z == 0.0, -1.0, jnp.where(step_z == 1.0, 1.0, 0.0))
        masses = [slot_row(xt_ref, c, b) for c in range(CH)]
        grads = []
        for k in range(3):
            sampled = jnp.dot(
                here[:, 0:208], planes[b, :, k * 512 : k * 512 + 512], preferred_element_type=F32
            )
            total = jnp.zeros((40, 512), F32)
            for c in range(CH):
                v = sampled[c * 48 : c * 48 + 40]
                if k == 0:
                    grads.append(jnp.sum(v * wz, axis=0, keepdims=True))
                total = total + masses[c] * v
            if k == 0:
                slope_z = jnp.sum(total * sz, axis=0, keepdims=True)
            else:
                grads.append(jnp.sum(total * wz, axis=0, keepdims=True))
        grads.append(slope_z)
        for r in range(7):
            ot[pl.ds(r * LANES + 2 * b, 1), :] = grads[r][:, 0:256]
            ot[pl.ds(r * LANES + 2 * b + 1, 1), :] = grads[r][:, 256:512]
        return carry

    lax.fori_loop(0, NZ // ZB, block, 0, unroll=16)
    for j in range(BACK):
        for h in range(2):
            piece = ot[j * 128 : j * 128 + 128, h * 128 : h * 128 + 128]
            tall[pl.ds(h * 128 * BACK + j, 128, stride=BACK), :] = piece.T
    out_ref[...] = tall[0 : TILES * BACK].astype(BF16)


def correlation(smoothing, rows, columns):
    distance = jnp.abs(rows - columns)
    distance = jnp.minimum(distance, NY - distance).astype(F32)
    breadth = smoothing
    profile = jnp.exp(-distance * distance / (2.0 * breadth * breadth)) / jnp.sqrt(breadth)
    return (profile + jnp.where(distance == 0.0, 1.0, 0.0)).astype(BF16)


def call(kernel, outs, scratch, mebibytes):
    return pl.pallas_call(
        kernel,
        out_shape=outs,
        scratch_shapes=scratch,
        compiler_params=params(mebibytes),
    )


def exchange(rows, wide, axes):
    rows = rows.reshape(TILES, wide, 2, 128).transpose(0, 2, 1, 3).reshape(TILES, 2, wide * 128)
    rows = lax.all_to_all(rows, axes, split_axis=0, concat_axis=0, tiled=True)
    rows = rows.reshape(TILES, 2, wide, 128).transpose(0, 2, 1, 3)
    return rows.reshape(TILES * 2 * wide, 128)


def shape(dims, kind):
    return jax.ShapeDtypeStruct(dims, kind)


def per_device(fractions, cell_index, weights, counts, smoothing, bias_values, observed, precision):
    both = ("slab", "pencil")
    count = lax.axis_size("slab")
    forth = [(i, (i + 1) % count) for i in range(count)]
    aft = [((i + 1) % count, i) for i in range(count)]

    ids = jnp.arange(NY, dtype=jnp.int32)
    breadth = smoothing[:, None, None]
    k_row = correlation(breadth, ids[None, :256, None], ids[None, None, :])
    k_col = correlation(breadth, ids[None, :, None], ids[None, None, :256])
    k_back = correlation(breadth, ids[None, :, None] - 1, ids[None, None, :256])
    rim = jnp.arange(128, dtype=jnp.int32)
    rim_y = (rim // 8 * TY - 1 + rim % 2 * (TY + 1)) % NY
    k_rim = correlation(smoothing[rim % 8 // 2][:, None], rim_y[:, None], ids[None, :])

    table = counts[0].T
    split = [a.reshape(a.shape[0], 128, 128).transpose(1, 0, 2) for a in (fractions, cell_index, weights)]
    mask = pltpu.VMEM((TILES + 8, 128), F32)
    records = call(
        pack_kernel,
        shape((TILES * PAIRS, 128), BF16),
        [pltpu.VMEM((TILES * PAIRS + 16, 128), F32), mask],
        56,
    )(*split, table)
    arrived = exchange(records, PAIRS // 2, both)
    arrived, k_row, k_col, k_back, k_rim = lax.optimization_barrier(
        (arrived, k_row, k_col, k_back, k_rim)
    )
    from_up = lax.ppermute(arrived, "slab", forth)
    from_dn = lax.ppermute(arrived, "slab", aft)
    turned = pltpu.VMEM((RECORD, TILES), F32)
    wide = pltpu.VMEM((TILES * PAIRS + 8, 128), F32)
    places = [pltpu.VMEM((72, 512), F32), pltpu.VMEM((40, 512), F32)]
    acc, xt = call(
        own_kernel,
        (shape((CH, 1040, 128), F32), shape((RECORD, TILES), F32)),
        [wide] + places,
        12,
    )(arrived)
    whole = pl.BlockSpec(memory_space=pltpu.VMEM)
    lines = pl.pallas_call(
        forward_kernel,
        out_shape=shape((N_PENCIL, CHUNK, 128), BF16),
        in_specs=[whole] * 3 + [pl.BlockSpec(memory_space=pltpu.HBM)],
        scratch_shapes=[pltpu.VMEM((CH, 1040, 128), F32), turned, wide]
        + places
        + [
            pltpu.VMEM((CH, NZ, 128), BF16),
            pltpu.VMEM((CH, NZ, 128), F32),
            pltpu.VMEM((CH, NZ, 256), BF16),
            pltpu.SemaphoreType.DMA,
        ],
        compiler_params=params(24),
    )(from_up, from_dn, acc, pltpu.with_memory_space_constraint(k_col, pltpu.HBM))
    lines = lax.all_to_all(lines, "pencil", split_axis=0, concat_axis=0, tiled=True)
    model_field, lines = pl.pallas_call(
        lines_kernel,
        out_shape=(shape((64, NY), BF16), shape((N_PENCIL, CHUNK, 128), BF16)),
        in_specs=[pl.BlockSpec(memory_space=pltpu.SMEM)] + [pl.BlockSpec(memory_space=pltpu.VMEM)] * 5,
        scratch_shapes=[pltpu.VMEM((CH, 256, 256), BF16), pltpu.VMEM((CH, 64, NY), F32)],
        compiler_params=params(20),
    )(bias_values, lines, k_row, k_rim, observed[0], precision[0])
    lines = lax.all_to_all(lines, "pencil", split_axis=0, concat_axis=0, tiled=True)
    fields = []
    for pair in range(2):
        field = call(
            functools.partial(adjoint_kernel, pair),
            shape((NZ + 64, 128), BF16),
            [pltpu.VMEM((2, NZ, 128), BF16), pltpu.VMEM((2, NZ, 128), F32)],
            16,
        )(lines, k_back)
        if pair == 1:
            field, late = lax.optimization_barrier((field, xt))
        fields += [field, lax.ppermute(field, "slab", forth), lax.ppermute(field, "slab", aft)]
    planes = pl.pallas_call(
        weights_kernel,
        out_shape=shape((NZ // ZB, 208, 1536), BF16),
        scratch_shapes=[pltpu.VMEM((72, 512), F32)],
        compiler_params=params(22),
        cost_estimate=pl.CostEstimate(flops=60_000_000, bytes_accessed=21_000_000, transcendentals=0),
    )(late)
    sampled = call(
        sample_kernel,
        shape((TILES * BACK, 128), BF16),
        [
            pltpu.VMEM((CH, NZ + 16, 256), BF16),
            pltpu.VMEM((BACK * 128, TILES), F32),
            pltpu.VMEM((TILES * BACK + 8, 128), F32),
        ],
        30,
    )(planes, xt, *fields)
    came_back = lax.all_to_all(
        sampled.reshape(TILES, BACK, 128), both, split_axis=0, concat_axis=0, tiled=True
    ).reshape(TILES * BACK, 128)
    grads = call(
        unpack_kernel,
        shape((128, 7, 128), F32),
        [pltpu.VMEM((TILES * BACK + 8, 128), F32), mask],
        12,
    )(came_back, table)
    return (grads.transpose(1, 0, 2).reshape(7, PART_DEV), model_field[None])


def solution(mesh):
    return jax.shard_map(
        per_device,
        mesh=mesh,
        in_specs=(
            P(None, ("slab", "pencil")),
            P(None, ("slab", "pencil")),
            P(None, ("slab", "pencil")),
            P(("slab", "pencil"), None, None),
            P(),
            P(),
            P("slab", "pencil", None),
            P("slab", "pencil", None),
        ),
        out_specs=(P(None, ("slab", "pencil")), P("slab", "pencil", None)),
        check_vma=False,
    )
```

```python
import jax
import jax.numpy as jnp
from jax import lax
from jax.experimental import pallas as pl
from jax.experimental.pallas import tpu as pltpu
from jax.sharding import PartitionSpec as P

NY = 1024
NZ = 1024
ZB = 32
PART_DEV = 16384
TILES = 256
CAP = 2
TY = 64
LANES = 64
RECORD = 12 * LANES
GRADS = 7 * LANES
CH = 4
N_PENCIL = 16
CHUNK = 136
F32 = jnp.float32
BF16 = jnp.bfloat16

R_GX, R_GY, R_GZ, R_LOW, R_CY, R_CZ = 4, 5, 6, 3, 10, 11


PAIRS = RECORD // 128
PART = NZ + 64
BACK = 4


def params(mebibytes):
    return pltpu.CompilerParams(vmem_limit_bytes=mebibytes * 1024 * 1024)


def lanes_of(shape):
    return lax.broadcasted_iota(jnp.int32, shape, len(shape) - 1)


def live_rows(counts_ref, scr):
    lane = lanes_of((ZB, 128))
    block = lax.broadcasted_iota(jnp.int32, (ZB, 128), 0)
    spread = jnp.where((lane % LANES) // CAP == block, 1.0, 0.0).astype(BF16)
    held = lax.dot_general(
        counts_ref[...].astype(F32).astype(BF16),
        spread,
        (((0,), (0,)), ((), ())),
        preferred_element_type=F32,
    )
    rank = (lanes_of((TILES, 128)) % CAP).astype(F32)
    scr[0:TILES] = jnp.where(rank < held, 1.0, 0.0)
    return scr[pl.ds(0, 128, stride=2), :] > 0.0, scr[pl.ds(1, 128, stride=2), :] > 0.0


def pack_kernel(fr_ref, ci_ref, wt_ref, cn_ref, out_ref, scr, mask):
    low = lanes_of((128, 128)) < LANES
    live = live_rows(cn_ref, mask)

    def put(k, a, b, masked=False):
        even = jnp.where(low, a, pltpu.roll(b, LANES, 1))
        odd = jnp.where(low, pltpu.roll(a, LANES, 1), b)
        if masked:
            even, odd = jnp.where(live[0], even, 0.0), jnp.where(live[1], odd, 0.0)
        scr[pl.ds(k, 128, stride=2 * PAIRS), :] = even
        scr[pl.ds(PAIRS + k, 128, stride=2 * PAIRS), :] = odd

    weights = wt_ref[...].astype(F32)
    put(0, weights[:, 0, :], weights[:, 1, :], True)
    put(1, weights[:, 2, :], weights[:, 3, :], True)
    offsets = [fr_ref[:, d, :] - 0.5 for d in range(3)]
    high = [g.astype(BF16).astype(F32) for g in offsets]
    rest = [g - h for g, h in zip(offsets, high)]
    put(2, high[0], high[1])
    put(3, high[2], rest[0])
    put(4, rest[1], rest[2])
    put(5, ci_ref[:, 1, :].astype(F32), ci_ref[:, 2, :].astype(F32))
    out_ref[...] = scr[0 : TILES * PAIRS].astype(BF16)


def unpack_kernel(in_ref, cn_ref, out_ref, scr, mask):
    low = lanes_of((128, 128)) < LANES
    live = live_rows(cn_ref, mask)
    scr[0 : TILES * BACK] = in_ref[...].astype(F32)
    for j in range(BACK):
        even = jnp.where(live[0], scr[pl.ds(j, 128, stride=2 * BACK), :], 0.0)
        odd = jnp.where(live[1], scr[pl.ds(BACK + j, 128, stride=2 * BACK), :], 0.0)
        out_ref[:, 2 * j, :] = jnp.where(low, even, pltpu.roll(odd, LANES, 1))
        if j < 3:
            out_ref[:, 2 * j + 1, :] = jnp.where(low, pltpu.roll(even, LANES, 1), odd)


def transpose_records(x_ref, wide, xt_ref):
    wide[0 : TILES * PAIRS] = x_ref[...].astype(F32)
    for k in range(PAIRS):
        for h in range(2):
            piece = wide[pl.ds(h * 128 * PAIRS + k, 128, stride=PAIRS), :]
            xt_ref[k * 128 : k * 128 + 128, h * 128 : h * 128 + 128] = piece.T
    first, last = R_GX * LANES, R_GZ * LANES + LANES
    xt_ref[first:last, :] += xt_ref[first + R_LOW * LANES : last + R_LOW * LANES, :]


def slot_row(xt_ref, r, b):
    first = xt_ref[pl.ds(r * LANES + 2 * b, 1), :]
    second = xt_ref[pl.ds(r * LANES + 2 * b + 1, 1), :]
    return jnp.concatenate([first, second], axis=1)


def hat(places, centre):
    return jnp.maximum(1.0 - jnp.abs(places - centre), 0.0)


def rim_places(rows):
    row = lax.broadcasted_iota(jnp.int32, (rows, 128), 0)
    y = jnp.where(row == 64, -1, jnp.where(row == 65, 64, jnp.where(row > 65, 1000, row)))
    return y.astype(F32)


def deposit(xt_ref, acc_ref, yv_ref, zv_ref, side):
    def block(b, carry):
        gx = slot_row(xt_ref, R_GX, b)
        if side == 0:
            wx = 1.0 - jnp.abs(gx)
        elif side < 0:
            wx = jnp.maximum(-gx, 0.0)
        else:
            wx = jnp.maximum(gx, 0.0)
        py = slot_row(xt_ref, R_CY, b) + slot_row(xt_ref, R_GY, b)
        pz = slot_row(xt_ref, R_CZ, b) + slot_row(xt_ref, R_GZ, b) + 1.0
        plane = (wx * hat(yv_ref[...], py)).astype(BF16)
        wz = hat(zv_ref[...], pz)
        column = jnp.concatenate([slot_row(xt_ref, c, b) * wz for c in range(CH)], axis=0).astype(BF16)
        add = lax.dot_general(column, plane, (((1,), (1,)), ((), ())), preferred_element_type=F32)
        at = pl.multiple_of(b * ZB, ZB)
        for c in range(CH):
            acc_ref[c, pl.ds(at, 40), 0:72] += add[c * 40 : c * 40 + 40]
        return carry

    lax.fori_loop(0, NZ // ZB, block, 0, unroll=32)


def fill_places(yv_ref, zv_ref):
    yv = rim_places(72)
    zv = lax.broadcasted_iota(jnp.int32, (40, 128), 0).astype(F32)
    for k in range(4):
        yv_ref[:, k * 128 : k * 128 + 128] = yv
        zv_ref[:, k * 128 : k * 128 + 128] = zv


def own_kernel(x_ref, acc_ref, xt_ref, wide, yv_ref, zv_ref):
    fill_places(yv_ref, zv_ref)
    transpose_records(x_ref, wide, xt_ref)
    acc_ref[...] = jnp.zeros_like(acc_ref)
    deposit(xt_ref, acc_ref, yv_ref, zv_ref, 0)


def along_z(field_ref, col_ref, out_ref, first, count):
    def channel(c, carry):
        quarters = [field_ref[c, i * 256 : i * 256 + 256, :] for i in range(4)]
        pairs = [jnp.concatenate(quarters[i : i + 2], axis=1) for i in (0, 2)]
        right = jnp.concatenate(pairs, axis=0)
        cols = [col_ref[first + c, d * 256 : d * 256 + 256, :] for d in range(4)]
        prods = [
            jnp.dot(
                jnp.concatenate([cols[d], cols[(d - 2) % 4]], axis=1),
                right,
                preferred_element_type=F32,
            )
            for d in range(4)
        ]
        for j in range(4):
            out_ref[c, j * 256 : j * 256 + 256, :] = prods[j][:, 0:128] + prods[(j - 1) % 4][:, 128:256]
        return carry

    lax.fori_loop(0, count, channel, 0, unroll=2)


def rim_rows(parts, rows):
    lane = lanes_of((rows, 128))
    table = jnp.zeros((rows, 128), F32)
    for c, part in enumerate(parts):
        table = jnp.where(lane // 2 == c, pltpu.roll(part, LANES + 2 * c, 1), table)
    return table.T[0:8]


def forward_kernel(up_ref, dn_ref, start_ref, col_ref, out_ref, acc, xt, wide, yv, zv, dens, smooth, cols, sem):
    fetch = pltpu.make_async_copy(col_ref, cols, sem)
    fetch.start()
    fill_places(yv, zv)
    acc[...] = start_ref[...]
    transpose_records(up_ref, wide, xt)
    deposit(xt, acc, yv, zv, 1)
    transpose_records(dn_ref, wide, xt)
    deposit(xt, acc, yv, zv, -1)
    acc[:, NZ : NZ + 1, :] += acc[:, 0:1, :]
    acc[:, 1:2, :] += acc[:, NZ + 1 : NZ + 2, :]
    dens[...] = acc[:, 1 : NZ + 1, :].astype(BF16)
    fetch.wait()
    along_z(dens, cols, smooth, 0, CH)
    low = lanes_of((64, 128)) < LANES

    def send(p, carry):
        at = pl.multiple_of(p * 64, 64)
        parts = [smooth[c, pl.ds(at, 64), :] for c in range(CH)]
        for pair in range(2):
            both = jnp.where(low, parts[2 * pair], pltpu.roll(parts[2 * pair + 1], LANES, 1))
            out_ref[p, pair * 64 : pair * 64 + 64, :] = both.astype(BF16)
        rims = rim_rows(parts, 64)
        out_ref[p, 128:136, :] = jnp.concatenate([rims, jnp.zeros((8, 64), F32)], axis=1).astype(BF16)
        return carry

    lax.fori_loop(0, N_PENCIL, send, 0, unroll=16)


def wrapped_sum(prod):
    blocks = []
    for j in range(4):
        total = prod[0:64, j * 256 : j * 256 + 256]
        for i in range(1, 4):
            d = (j - i) % 4
            total = total + prod[i * 64 : i * 64 + 64, d * 256 : d * 256 + 256]
        blocks.append(total)
    return jnp.concatenate(blocks, axis=1)


def lines_kernel(bias_ref, in_ref, row_ref, rim_ref, obs_ref, prec_ref, model_ref, out_ref, left, back):
    low = lanes_of((64, 128)) < LANES
    for pair in range(2):
        for pp in range(8):
            a = in_ref[2 * pp, pair * 64 : pair * 64 + 64, :].astype(F32)
            b = in_ref[2 * pp + 1, pair * 64 : pair * 64 + 64, :].astype(F32)
            i, at = pp // 2, (pp % 2) * 128
            left[2 * pair, i * 64 : i * 64 + 64, at : at + 128] = jnp.where(
                low, a, pltpu.roll(b, LANES, 1)
            ).astype(BF16)
            left[2 * pair + 1, i * 64 : i * 64 + 64, at : at + 128] = jnp.where(
                low, pltpu.roll(a, LANES, 1), b
            ).astype(BF16)
    which = lax.broadcasted_iota(jnp.int32, (128, 64), 0) % 8 // 2
    bias = jnp.zeros((128, 64), F32)
    for c in range(CH):
        bias = jnp.where(which == c, bias_ref[c], bias)
    rims = jnp.concatenate([in_ref[p, 128:136, 0:64].astype(F32) for p in range(N_PENCIL)], axis=0)
    rims = (rims * bias).T.astype(BF16)
    model = jnp.dot(rims, rim_ref[...], preferred_element_type=F32)
    for c in range(CH):
        prod = jnp.dot(left[c], row_ref[c], preferred_element_type=F32)
        model = model + bias_ref[c] * wrapped_sum(prod)
    model_ref[...] = model.astype(BF16)
    pull = (prec_ref[...] * (model - obs_ref[...])).astype(BF16)
    stacked = jnp.concatenate([pull[:, i * 256 : i * 256 + 256] for i in range(4)], axis=0)
    for c in range(CH):
        prod = jnp.dot(stacked, row_ref[c], preferred_element_type=F32)
        back[c] = bias_ref[c] * wrapped_sum(prod)
    for pair in range(2):
        for pp in range(8):
            a = back[2 * pair, :, pp * 128 : pp * 128 + 128]
            b = back[2 * pair + 1, :, pp * 128 : pp * 128 + 128]
            out_ref[2 * pp, pair * 64 : pair * 64 + 64, :] = jnp.where(
                low, a, pltpu.roll(b, LANES, 1)
            ).astype(BF16)
            out_ref[2 * pp + 1, pair * 64 : pair * 64 + 64, :] = jnp.where(
                low, pltpu.roll(a, LANES, 1), b
            ).astype(BF16)
    rims = lax.dot_general(rim_ref[...], pull, (((1,), (1,)), ((), ())), preferred_element_type=F32)
    rims = jnp.concatenate([rims * bias, jnp.zeros((128, 64), F32)], axis=1).astype(BF16)
    for p in range(N_PENCIL):
        out_ref[p, 128:136, :] = rims[p * 8 : p * 8 + 8]


def adjoint_kernel(in_ref, col_ref, out_ref, field, smooth):
    lane = lanes_of((64, 128))
    low = lane < LANES

    def take(p, carry):
        at = pl.multiple_of(p * 64, 64)
        rims = in_ref[p, 128:136, :].astype(F32)
        table = jnp.concatenate([rims, jnp.zeros((120, 128), F32)], axis=0).T[0:64]
        for pair in range(2):
            both = in_ref[p, pair * 64 : pair * 64 + 64, :].astype(F32)
            for k in range(2):
                c = 2 * pair + k
                main = both if k == 0 else pltpu.roll(both, LANES, 1)
                rim = jnp.where(lane < 66, pltpu.roll(table, LANES - 2 * c, 1), 0.0)
                field[c, pl.ds(at, 64), :] = jnp.where(low, main, rim).astype(BF16)
        return carry

    lax.fori_loop(0, N_PENCIL, take, 0, unroll=16)
    along_z(field, col_ref, smooth, 0, CH)
    wide = lanes_of((128, 128)) < LANES
    for pair in range(2):
        base = pair * PART
        for q in range(8):
            parts = [smooth[2 * pair + k, q * 128 : q * 128 + 128, :] for k in range(2)]
            both = jnp.where(wide, parts[0], pltpu.roll(parts[1], LANES, 1))
            out_ref[base + q * 128 : base + q * 128 + 128, :] = both.astype(BF16)
            out_ref[base + NZ + q * 8 : base + NZ + q * 8 + 8, :] = rim_rows(parts, 128).astype(BF16)


def write_planes(xt_ref, b, places, planes):
    gx, gy, cy = (slot_row(xt_ref, r, b) for r in (R_GX, R_GY, R_CY))
    fall_x, fall_y = gx < 0.0, gy < 0.0
    wx = [jnp.maximum(-gx, 0.0), jnp.maximum(gx, 0.0), 1.0 - jnp.abs(gx)]
    sx = [jnp.where(fall_x, -1.0, 0.0), jnp.where(fall_x, 0.0, 1.0), jnp.where(fall_x, 1.0, -1.0)]
    wy = hat(places, cy + gy)
    step_y = places - jnp.where(fall_y, cy - 1.0, cy)
    sy = jnp.where(step_y == 0.0, -1.0, jnp.where(step_y == 1.0, 1.0, 0.0))
    wx16, sx16 = ([a.astype(BF16) for a in ax] for ax in (wx, sx))
    wy16, sy16 = wy[0:64].astype(BF16), sy[0:64].astype(BF16)
    for s in range(3):
        rows = slice(s * 64, s * 64 + 64)
        planes[rows, 0:512] = (wx[s] * wy[0:64]).astype(BF16)
        planes[rows, 512:1024] = sx16[s] * wy16
        planes[rows, 1024:1536] = wx16[s] * sy16
    part = lax.broadcasted_iota(jnp.int32, (8, 512), 0) // 2
    for k, (ax, ay) in enumerate(((wx, wy), (sx, wy), (wx, sy))):
        rim = jnp.where(
            part == 0, ax[2], jnp.where(part == 1, ax[0], jnp.where(part == 2, ax[1], 0.0))
        )
        rim = jnp.concatenate([rim * ay[64:72], jnp.zeros((8, 512), F32)], axis=0)
        planes[192:208, k * 512 : k * 512 + 512] = rim.astype(BF16)


def weights_kernel(xt_ref, planes, yv):
    row = lax.broadcasted_iota(jnp.int32, (72, 512), 0)
    yv[...] = jnp.where(row < 64, row, jnp.where(row % 2 == 0, -1, 64)).astype(F32)

    def block(b, carry):
        write_planes(xt_ref, b, yv[...], planes.at[b])
        return carry

    lax.fori_loop(0, NZ // ZB, block, 0, unroll=2)


def fill_field(refs, field):
    lane = lanes_of((128, 128))
    low = lane < LANES

    def fill(q, carry):
        at = pl.multiple_of(q * 128, 128)
        for pair in range(2):
            rim_at = pl.multiple_of(pair * PART + NZ + q * 8, 8)
            tables = []
            for ref in refs:
                rims = ref[pl.ds(rim_at, 8), :].astype(F32)
                tables.append(jnp.concatenate([rims, jnp.zeros((120, 128), F32)], axis=0).T)
            own, up, dn = (ref[pl.ds(pair * PART + at, 128), :].astype(F32) for ref in refs)
            for k in range(2):
                c = 2 * pair + k
                if k == 0:
                    first = jnp.where(low, up, pltpu.roll(dn, LANES, 1))
                    main = own
                else:
                    first = jnp.where(low, pltpu.roll(up, LANES, 1), dn)
                    main = pltpu.roll(own, LANES, 1)
                rim = jnp.zeros((128, 128), F32)
                for s in range(3):
                    here = pltpu.roll(tables[s], LANES + 2 * s - 2 * k, 1)
                    rim = jnp.where((lane - LANES) // 2 == s, here, rim)
                field[c, pl.ds(at, 128), 0:128] = first.astype(BF16)
                field[c, pl.ds(at, 128), 128:256] = jnp.where(low, main, rim).astype(BF16)
        return carry

    lax.fori_loop(0, 8, fill, 0, unroll=8)
    field[:, NZ : NZ + 16, :] = field[:, 0:16, :]


def sample_kernel(planes, xt_ref, *rest):
    refs, (out_ref, field, ot, tall) = rest[0:3], rest[3:]
    fill_field(refs, field)
    zv = lax.broadcasted_iota(jnp.int32, (40, 512), 0).astype(F32)
    ot[GRADS:, :] = jnp.zeros((LANES, TILES), F32)

    def block(b, carry):
        gz, cz = slot_row(xt_ref, R_GZ, b), slot_row(xt_ref, R_CZ, b)
        at = pl.multiple_of(b * ZB, ZB)
        here = jnp.concatenate([field[c, pl.ds(at, 48), :] for c in range(CH)], axis=0)
        wz = hat(zv, cz + gz + 1.0)
        step_z = zv - jnp.where(gz < 0.0, cz, cz + 1.0)
        sz = jnp.where(step_z == 0.0, -1.0, jnp.where(step_z == 1.0, 1.0, 0.0))
        masses = [slot_row(xt_ref, c, b) for c in range(CH)]
        grads = []
        for k in range(3):
            sampled = jnp.dot(
                here[:, 0:208], planes[b, :, k * 512 : k * 512 + 512], preferred_element_type=F32
            )
            total = jnp.zeros((40, 512), F32)
            for c in range(CH):
                v = sampled[c * 48 : c * 48 + 40]
                if k == 0:
                    grads.append(jnp.sum(v * wz, axis=0, keepdims=True))
                total = total + masses[c] * v
            if k == 0:
                slope_z = jnp.sum(total * sz, axis=0, keepdims=True)
            else:
                grads.append(jnp.sum(total * wz, axis=0, keepdims=True))
        grads.append(slope_z)
        for r in range(7):
            ot[pl.ds(r * LANES + 2 * b, 1), :] = grads[r][:, 0:256]
            ot[pl.ds(r * LANES + 2 * b + 1, 1), :] = grads[r][:, 256:512]
        return carry

    lax.fori_loop(0, NZ // ZB, block, 0, unroll=16)
    for j in range(BACK):
        for h in range(2):
            piece = ot[j * 128 : j * 128 + 128, h * 128 : h * 128 + 128]
            tall[pl.ds(h * 128 * BACK + j, 128, stride=BACK), :] = piece.T
    out_ref[...] = tall[0 : TILES * BACK].astype(BF16)


def correlation(smoothing, rows, columns):
    distance = jnp.abs(rows - columns)
    distance = jnp.minimum(distance, NY - distance).astype(F32)
    breadth = smoothing
    profile = jnp.exp(-distance * distance / (2.0 * breadth * breadth)) / jnp.sqrt(breadth)
    return (profile + jnp.where(distance == 0.0, 1.0, 0.0)).astype(BF16)


def call(kernel, outs, scratch, mebibytes):
    return pl.pallas_call(
        kernel,
        out_shape=outs,
        scratch_shapes=scratch,
        compiler_params=params(mebibytes),
    )


def exchange(rows, wide, axes):
    rows = rows.reshape(TILES, wide, 2, 128).transpose(0, 2, 1, 3).reshape(TILES, 2, wide * 128)
    rows = lax.all_to_all(rows, axes, split_axis=0, concat_axis=0, tiled=True)
    rows = rows.reshape(TILES, 2, wide, 128).transpose(0, 2, 1, 3)
    return rows.reshape(TILES * 2 * wide, 128)


def shape(dims, kind):
    return jax.ShapeDtypeStruct(dims, kind)


def per_device(fractions, cell_index, weights, counts, smoothing, bias_values, observed, precision):
    both = ("slab", "pencil")
    count = lax.axis_size("slab")
    forth = [(i, (i + 1) % count) for i in range(count)]
    aft = [((i + 1) % count, i) for i in range(count)]

    ids = jnp.arange(NY, dtype=jnp.int32)
    breadth = smoothing[:, None, None]
    k_row = correlation(breadth, ids[None, :256, None], ids[None, None, :])
    k_col = correlation(breadth, ids[None, :, None], ids[None, None, :256])
    k_back = correlation(breadth, ids[None, :, None] - 1, ids[None, None, :256])
    rim = jnp.arange(128, dtype=jnp.int32)
    rim_y = (rim // 8 * TY - 1 + rim % 2 * (TY + 1)) % NY
    k_rim = correlation(smoothing[rim % 8 // 2][:, None], rim_y[:, None], ids[None, :])

    table = counts[0].T
    split = [a.reshape(a.shape[0], 128, 128).transpose(1, 0, 2) for a in (fractions, cell_index, weights)]
    mask = pltpu.VMEM((TILES + 8, 128), F32)
    records = call(
        pack_kernel,
        shape((TILES * PAIRS, 128), BF16),
        [pltpu.VMEM((TILES * PAIRS + 16, 128), F32), mask],
        56,
    )(*split, table)
    arrived = exchange(records, PAIRS // 2, both)
    arrived, k_row, k_col, k_back, k_rim = lax.optimization_barrier(
        (arrived, k_row, k_col, k_back, k_rim)
    )
    from_up = lax.ppermute(arrived, "slab", forth)
    from_dn = lax.ppermute(arrived, "slab", aft)
    turned = pltpu.VMEM((RECORD, TILES), F32)
    wide = pltpu.VMEM((TILES * PAIRS + 8, 128), F32)
    places = [pltpu.VMEM((72, 512), F32), pltpu.VMEM((40, 512), F32)]
    acc, xt = call(
        own_kernel,
        (shape((CH, 1040, 128), F32), shape((RECORD, TILES), F32)),
        [wide] + places,
        12,
    )(arrived)
    whole = pl.BlockSpec(memory_space=pltpu.VMEM)
    lines = pl.pallas_call(
        forward_kernel,
        out_shape=shape((N_PENCIL, CHUNK, 128), BF16),
        in_specs=[whole] * 3 + [pl.BlockSpec(memory_space=pltpu.HBM)],
        scratch_shapes=[pltpu.VMEM((CH, 1040, 128), F32), turned, wide]
        + places
        + [
            pltpu.VMEM((CH, NZ, 128), BF16),
            pltpu.VMEM((CH, NZ, 128), F32),
            pltpu.VMEM((CH, NZ, 256), BF16),
            pltpu.SemaphoreType.DMA,
        ],
        compiler_params=params(24),
    )(from_up, from_dn, acc, pltpu.with_memory_space_constraint(k_col, pltpu.HBM))
    lines = lax.all_to_all(lines, "pencil", split_axis=0, concat_axis=0, tiled=True)
    model_field, lines = pl.pallas_call(
        lines_kernel,
        out_shape=(shape((64, NY), BF16), shape((N_PENCIL, CHUNK, 128), BF16)),
        in_specs=[pl.BlockSpec(memory_space=pltpu.SMEM)] + [pl.BlockSpec(memory_space=pltpu.VMEM)] * 5,
        scratch_shapes=[pltpu.VMEM((CH, 256, 256), BF16), pltpu.VMEM((CH, 64, NY), F32)],
        compiler_params=params(20),
    )(bias_values, lines, k_row, k_rim, observed[0], precision[0])
    lines = lax.all_to_all(lines, "pencil", split_axis=0, concat_axis=0, tiled=True)
    field = call(
        adjoint_kernel,
        shape((2 * PART, 128), BF16),
        [pltpu.VMEM((CH, NZ, 128), BF16), pltpu.VMEM((CH, NZ, 128), F32)],
        16,
    )(lines, k_back)
    field, late = lax.optimization_barrier((field, xt))
    fields = [field, lax.ppermute(field, "slab", forth), lax.ppermute(field, "slab", aft)]
    planes = pl.pallas_call(
        weights_kernel,
        out_shape=shape((NZ // ZB, 208, 1536), BF16),
        scratch_shapes=[pltpu.VMEM((72, 512), F32)],
        compiler_params=params(22),
        cost_estimate=pl.CostEstimate(flops=60_000_000, bytes_accessed=21_000_000, transcendentals=0),
    )(late)
    sampled = call(
        sample_kernel,
        shape((TILES * BACK, 128), BF16),
        [
            pltpu.VMEM((CH, NZ + 16, 256), BF16),
            pltpu.VMEM((BACK * 128, TILES), F32),
            pltpu.VMEM((TILES * BACK + 8, 128), F32),
        ],
        30,
    )(planes, xt, *fields)
    came_back = lax.all_to_all(
        sampled.reshape(TILES, BACK, 128), both, split_axis=0, concat_axis=0, tiled=True
    ).reshape(TILES * BACK, 128)
    grads = call(
        unpack_kernel,
        shape((128, 7, 128), F32),
        [pltpu.VMEM((TILES * BACK + 8, 128), F32), mask],
        12,
    )(came_back, table)
    return (grads.transpose(1, 0, 2).reshape(7, PART_DEV), model_field[None])


def solution(mesh):
    return jax.shard_map(
        per_device,
        mesh=mesh,
        in_specs=(
            P(None, ("slab", "pencil")),
            P(None, ("slab", "pencil")),
            P(None, ("slab", "pencil")),
            P(("slab", "pencil"), None, None),
            P(),
            P(),
            P("slab", "pencil", None),
            P("slab", "pencil", None),
        ),
        out_specs=(P(None, ("slab", "pencil")), P("slab", "pencil", None)),
        check_vma=False,
    )
```
